32 devices in a mesh: gx: 4 (over y, core), gy: 4 (over z), gz: 2 (over x).
Axes of the slice: x: 2, y: 2, z: 4, core: 2. Of those that a mesh axis runs over, the one named last changes fastest.
Arguments:
- positions: float32 [4, 16, 2, 3, 128], P('gx', 'gy', 'gz'), may hold values from 0 to 1
- velocities: float32 [4, 16, 2, 3, 128], P('gx', 'gy', 'gz'), may hold values from -6 to 6
- charges: float32 [4, 16, 2, 128], P('gx', 'gy', 'gz'), may hold values from -3 to 3
- atom_types: int32 [4, 16, 2, 128], P('gx', 'gy', 'gz'), may hold values from 0 to 15
- atom_count: int32 [4, 16, 2], P('gx', 'gy', 'gz'), may hold values from 32 to 128
- sigma_type: float32 [16], replicated, may hold values from 0.15 to 0.35
- epsilon_type: float32 [16], replicated, may hold values from 0.3 to 3
- masses: float32 [4, 16, 2, 128], P('gx', 'gy', 'gz'), may hold values from 1 to 4
- pair_list: int32 [4, 4, 2, 2, 56], P('gx', 'gy', 'gz'), may hold values from 0 to 19, as said below
- pair_count: int32 [4, 4, 2], P('gx', 'gy', 'gz'), may hold values from 1 to 56, as said below
- pos_cotangent: float32 [4, 16, 2, 3, 128], P('gx', 'gy', 'gz'), may hold values from -6 to 6
- vel_cotangent: float32 [4, 16, 2, 3, 128], P('gx', 'gy', 'gz'), may hold values from -6 to 6
Outputs:
- pos_final: float32 [4, 16, 2, 3, 128], P('gx', 'gy', 'gz')
- vel_final: float32 [4, 16, 2, 3, 128], P('gx', 'gy', 'gz')
- grad_pos: float32 [4, 16, 2, 3, 128], P('gx', 'gy', 'gz')
- grad_vel: float32 [4, 16, 2, 3, 128], P('gx', 'gy', 'gz')
- grad_charge: float32 [4, 16, 2, 128], P('gx', 'gy', 'gz')
The draws below stay inside these ranges and needn't reach their ends.
Inputs may be any that keep to these rules, and one draw needn't show every extreme that they name: `pair_list`: for k < pair_count[a, b, c] the two extended indices of slot k name blocks inside the global grid of 4 x 16 x 2 blocks, their coordinates differ by at most one in each dimension, and their smaller coordinate in each dimension lies in the device's own blocks; an unordered pair of blocks appears in at most one live slot over all devices. Slots at and past the count hold indices in range and are ignored. `pair_count`: some device has all 56 slots live in every draw.
All inputs are finite; a program needn't handle non-finite values.
Results may differ from the reference program's by a relative error of at most 0.00027.
Values sent between devices are 32-bit elements; how exact they have to be, the bound alone decides.
A program may use at most 64 MiB of HBM per device.

```python
import math
import jax
import jax.numpy as jnp
import numpy as np
from jax import lax

BX = 1
BY = 4
BZ = 1
ATOMS = 128
NTYPES = 16
STEPS = 5
NX = 4
NY = 16
NZ = 2


def corner_pairs():
    options = ((0, 0), (0, 1), (1, 0))
    lefts = []
    rights = []
    for option_x in options:
        for option_y in options:
            for option_z in options:
                left_corner = (option_x[0], option_y[0], option_z[0])
                right_corner = (option_x[1], option_y[1], option_z[1])
                if left_corner <= right_corner:
                    lefts.append(left_corner)
                    rights.append(right_corner)
    return (np.array(lefts, dtype=np.int32), np.array(rights, dtype=np.int32))


def pair_tables(key):
    grid_x = NX // BX
    grid_y = NY // BY
    grid_z = NZ // BZ
    lefts, rights = corner_pairs()
    own_cells = np.array([[cell_x, cell_y, cell_z] for cell_x in range(BX) for cell_y in range(BY) for cell_z in range(BZ)], dtype=np.int32)
    cand_left = (own_cells[:, None, :] + lefts[None, :, :]).reshape(-1, 3)
    cand_right = (own_cells[:, None, :] + rights[None, :, :]).reshape(-1, 3)
    slot_total = cand_left.shape[0]

    def ext_index(coords):
        return ((coords[:, 0] * (BY + 1) + coords[:, 1]) * (BZ + 1) + coords[:, 2]).astype(np.int32)
    anchors = np.array([[dev_x * BX, dev_y * BY, dev_z * BZ] for dev_x in range(grid_x) for dev_y in range(grid_y) for dev_z in range(grid_z)], dtype=np.int32)
    highest = jnp.maximum(jnp.asarray(cand_left), jnp.asarray(cand_right))
    limits = jnp.asarray(np.array([NX, NY, NZ], dtype=np.int32))
    inside = jnp.all(jnp.asarray(anchors)[:, None, :] + highest[None, :, :] < limits, axis=-1)
    inside_total = jnp.sum(inside.astype(jnp.int32), axis=1).astype(jnp.int32)
    device_total = anchors.shape[0]
    shuffled = jax.vmap(lambda sub_key: jax.random.permutation(sub_key, slot_total))(jax.random.split(jax.random.fold_in(key, 11), device_total))
    scores = (jnp.where(inside, 0, slot_total) + shuffled).astype(jnp.int32)
    ordering = jnp.argsort(scores, axis=1, stable=True)
    left_ids = jnp.asarray(ext_index(cand_left))[ordering]
    right_ids = jnp.asarray(ext_index(cand_right))[ordering]
    reversal = jax.random.randint(jax.random.fold_in(key, 12), (device_total, slot_total), 0, 2)
    firsts = jnp.where(reversal == 1, right_ids, left_ids)
    seconds = jnp.where(reversal == 1, left_ids, right_ids)
    levels = jax.random.randint(jax.random.fold_in(key, 13), (device_total,), 1, 9)
    counts = jnp.maximum(slot_total * levels * levels // 64, 1)
    counts = jnp.minimum(counts, inside_total)
    counts = counts.at[device_total - 1].set(1)
    counts = counts.at[0].set(inside_total[0])
    return (firsts, seconds, counts, (grid_x, grid_y, grid_z, slot_total))


def draw_pair_list(key, part):
    firsts, seconds, counts, extents = pair_tables(key)
    stacked = jnp.stack([firsts, seconds], axis=1)
    return stacked.reshape(extents[0], extents[1], extents[2], 2, extents[3]).astype(jnp.int32)


def draw_pair_count(key, part):
    firsts, seconds, counts, extents = pair_tables(key)
    return counts.reshape(extents[0], extents[1], extents[2]).astype(jnp.int32)


def with_ends(values, own_key, smallest, high):
    spot = [jax.random.randint(jax.random.fold_in(own_key, axis), (), 0, length) for axis, length in enumerate(values.shape)]
    main_axis = values.shape.index(max(values.shape))
    next_to = spot[:main_axis] + [(spot[main_axis] + 1) % values.shape[main_axis]] + spot[main_axis + 1:]
    return values.at[tuple(spot)].set(smallest).at[tuple(next_to)].set(high)


def block_scale(rng, shape, pieces, least, high):
    def one(dim, blocks):
        heights = jax.random.uniform(jax.random.fold_in(jax.random.fold_in(rng, 6), dim), (blocks,), jnp.float32, least / len(pieces), high / len(pieces))
        return jnp.repeat(jnp.exp(heights), shape[dim] // blocks).reshape((-1,) + (1,) * (len(shape) - dim - 1))

    gain = one(*pieces[0])
    for cut in pieces[1:]:
        gain = gain * one(*cut)
    return gain


def noise(rng, shape, deviation, reach, pieces=(), kind=jnp.bfloat16):
    result = deviation * jax.random.normal(rng, shape, jnp.float32)
    if pieces:
        result = result * block_scale(rng, shape, pieces, -0.22, 0.18)
    return jnp.clip(result, -reach, reach).astype(kind)


def setup_inputs(seed: int = 0) -> dict:
    key_list = jax.random.split(jax.random.key(seed), 13)
    return {
        "positions": jnp.clip(1.0 * jax.random.uniform(key_list[0], (NX, NY, NZ, 3, ATOMS), jnp.float32) ** block_scale(key_list[0], (NX, NY, NZ, 3, ATOMS), ((0, 4), (1, 4), (2, 2)), -0.2, 0.2), 0.0, 1.0),
        "velocities": noise(key_list[1], (NX, NY, NZ, 3, ATOMS), 1.0, 6.0, ((0, 4), (1, 4), (2, 2)), jnp.float32),
        "charges": noise(key_list[2], (NX, NY, NZ, ATOMS), 0.5, 3.0, ((0, 4), (1, 4), (2, 2)), jnp.float32),
        "atom_types": with_ends(jax.random.randint(key_list[3], (NX, NY, NZ, ATOMS), 0, NTYPES), jax.random.fold_in(key_list[3], 1), 0, NTYPES - 1).astype(jnp.int32),
        "atom_count": with_ends(jax.random.randint(key_list[4], (NX, NY, NZ), ATOMS // 4, ATOMS + 1), jax.random.fold_in(key_list[4], 1), ATOMS // 4, ATOMS).astype(jnp.int32),
        "sigma_type": jnp.clip(jnp.exp(jax.random.uniform(key_list[5], (NTYPES,), jnp.float32, math.log(0.15), math.log(0.35))), 0.15, 0.35),
        "epsilon_type": jnp.clip(jnp.exp(jax.random.uniform(key_list[6], (NTYPES,), jnp.float32, math.log(0.3), math.log(3.0))), 0.3, 3.0),
        "masses": jnp.clip(jnp.exp(math.log(4.0) - 1.3862944 * jax.random.uniform(key_list[7], (NX, NY, NZ, ATOMS), jnp.float32) ** block_scale(key_list[7], (NX, NY, NZ, ATOMS), ((0, 4), (1, 4), (2, 2)), -0.2, 0.2)), 1.0, 4.0),
        "pair_list": draw_pair_list(jax.random.fold_in(key_list[12], 71), 0),
        "pair_count": draw_pair_count(jax.random.fold_in(key_list[12], 71), 0),
        "pos_cotangent": noise(key_list[10], (NX, NY, NZ, 3, ATOMS), 1.0, 6.0, ((0, 4), (1, 4), (2, 2)), jnp.float32),
        "vel_cotangent": noise(key_list[11], (NX, NY, NZ, 3, ATOMS), 1.0, 6.0, ((0, 4), (1, 4), (2, 2)), jnp.float32),
    }


SOFT = 0.04
KAPPA = 2.0
COULOMB = 4.0
TIME_STEP = 0.004

def tile_energy(left_pos, right_pos, left_charge, right_charge, left_sigma, right_sigma, left_depth, right_depth, offset, same_block):
    separation = left_pos[:, :, None] - right_pos[:, None, :] + offset[:, None, None]
    distance = lax.optimization_barrier(jnp.sum(separation * separation, axis=0))
    mean_sigma = 0.5 * (left_sigma[:, None] + right_sigma[None, :])
    squared_sigma = mean_sigma * mean_sigma
    fraction = squared_sigma / (distance + squared_sigma)
    third_power = fraction * fraction * fraction
    dispersion = 4.0 * left_depth[:, None] * right_depth[None, :] * (third_power * third_power - third_power)
    radius = jnp.sqrt(distance + SOFT)
    screened = COULOMB * left_charge[:, None] * right_charge[None, :] * jnp.exp(-KAPPA * radius) / radius
    fading = jnp.maximum(1.0 - distance, 0.0)
    switch = fading * fading * fading
    per_block = left_pos.shape[1]
    diagonal = (lax.broadcasted_iota(jnp.int32, (per_block, per_block), 0) == lax.broadcasted_iota(jnp.int32, (per_block, per_block), 1)).astype(jnp.float32)
    weight = 1.0 - same_block * (0.5 + 0.5 * diagonal)
    return jnp.sum(weight * switch * (dispersion + screened))

def tile_forces(left_pos, right_pos, left_charge, right_charge, left_sigma, right_sigma, left_depth, right_depth, offset, same_block):
    gradients = jax.grad(tile_energy, argnums=(0, 1))(left_pos, right_pos, left_charge, right_charge, left_sigma, right_sigma, left_depth, right_depth, offset, same_block)
    return (-gradients[0], -gradients[1])

def pair_terms(flat_pos, flat_par, flat_cot, first_ids, second_ids, offset, same_block, live_slot, with_forces):
    left_pos = jnp.take(flat_pos, first_ids, axis=0)
    right_pos = jnp.take(flat_pos, second_ids, axis=0)
    left_par = jnp.take(flat_par, first_ids, axis=0)
    right_par = jnp.take(flat_par, second_ids, axis=0)
    slot_mask = live_slot[:, None, None]

    def batch_forces(pos_one, pos_two, charge_one, charge_two):
        return jax.vmap(tile_forces)(pos_one, pos_two, charge_one, charge_two, left_par[:, 1], right_par[:, 1], left_par[:, 2], right_par[:, 2], offset, same_block)
    if flat_cot is None:
        left_force, right_force = batch_forces(left_pos, right_pos, left_par[:, 0], right_par[:, 0])
        return (left_force * slot_mask, right_force * slot_mask)
    results, pullback = jax.vjp(batch_forces, left_pos, right_pos, left_par[:, 0], right_par[:, 0])
    left_cot = jnp.take(flat_cot, first_ids, axis=0) * slot_mask
    right_cot = jnp.take(flat_cot, second_ids, axis=0) * slot_mask
    pulled = pullback((left_cot, right_cot))
    left_rows = [pulled[0], pulled[2][:, None, :]]
    right_rows = [pulled[1], pulled[3][:, None, :]]
    if with_forces:
        left_rows = [results[0] * slot_mask] + left_rows
        right_rows = [results[1] * slot_mask] + right_rows
    return (jnp.concatenate(left_rows, axis=1), jnp.concatenate(right_rows, axis=1))

def atom_params(charges, atom_types, atom_count, sigma_type, epsilon_type):
    type_total = sigma_type.shape[0]
    alive_mask = (lax.broadcasted_iota(jnp.int32, charges.shape, charges.ndim - 1) < atom_count[..., None]).astype(jnp.float32)
    matches = (atom_types[..., None, :] == lax.broadcasted_iota(jnp.int32, (type_total, 1), 0)).astype(jnp.float32)
    sigma_atom = lax.optimization_barrier(jnp.sum(matches * sigma_type[:, None], axis=-2))
    depth_atom = lax.optimization_barrier(jnp.sum(matches * epsilon_type[:, None], axis=-2))
    params = jnp.stack([charges * alive_mask, sigma_atom, jnp.sqrt(depth_atom) * alive_mask], axis=-2)
    return (alive_mask, params)

def global_pairs(pair_list, pair_count):
    grid_x, grid_y, grid_z, unused, slot_total = pair_list.shape
    grid_shape = (grid_x, grid_y, grid_z, slot_total)

    def local_coords(index):
        return (index // ((BY + 1) * (BZ + 1)), index // (BZ + 1) % (BY + 1), index % (BZ + 1))
    anchor_x = lax.broadcasted_iota(jnp.int32, grid_shape, 0) * BX
    anchor_y = lax.broadcasted_iota(jnp.int32, grid_shape, 1) * BY
    anchor_z = lax.broadcasted_iota(jnp.int32, grid_shape, 2) * BZ
    left_local = local_coords(pair_list[:, :, :, 0, :])
    right_local = local_coords(pair_list[:, :, :, 1, :])

    def global_index(coords):
        return ((coords[0] + anchor_x) * NY + (coords[1] + anchor_y)) * NZ + (coords[2] + anchor_z)
    live_grid = lax.broadcasted_iota(jnp.int32, grid_shape, 3) < pair_count[..., None]
    zero_ids = jnp.zeros(grid_shape, jnp.int32)
    first_ids = jnp.where(live_grid, global_index(left_local).astype(jnp.int32), zero_ids).astype(jnp.int32).reshape(-1)
    second_ids = jnp.where(live_grid, global_index(right_local).astype(jnp.int32), zero_ids).astype(jnp.int32).reshape(-1)
    offsets = jnp.stack([(left_local[column] - right_local[column]).astype(jnp.float32) for column in range(3)], axis=-1).reshape(-1, 3)
    same_block = (pair_list[:, :, :, 0, :] == pair_list[:, :, :, 1, :]).astype(jnp.float32).reshape(-1)
    live_slot = live_grid.astype(jnp.float32).reshape(-1)
    return (first_ids, second_ids, offsets, same_block, live_slot)

def reference(positions, velocities, charges, atom_types, atom_count, sigma_type, epsilon_type, masses, pair_list, pair_count, pos_cotangent, vel_cotangent):
    alive_mask, params = atom_params(charges, atom_types, atom_count, sigma_type, epsilon_type)
    blocks_total = NX * NY * NZ
    per_block = positions.shape[-1]
    flat_par = params.reshape(blocks_total, 3, per_block)
    first_ids, second_ids, offsets, same_block, live_slot = global_pairs(pair_list, pair_count)
    group = pair_list.shape[-1]
    batches = (first_ids.reshape(-1, group), second_ids.reshape(-1, group), offsets.reshape(-1, group, 3), same_block.reshape(-1, group), live_slot.reshape(-1, group))

    def evaluate(flat_pos, flat_cot):
        rows_total = 3 if flat_cot is None else 4

        def one_batch(totals, batch):
            first_batch, second_batch, offset_batch, same_batch, slot_batch = batch
            left_rows, right_rows = pair_terms(flat_pos, flat_par, flat_cot, first_batch, second_batch, offset_batch, same_batch, slot_batch, False)
            totals = totals.at[first_batch].add(left_rows).at[second_batch].add(right_rows)
            return (totals, None)
        totals, unused = lax.scan(one_batch, jnp.zeros((blocks_total, rows_total, per_block), jnp.float32), batches)
        return totals
    inverse = (1.0 / masses).reshape(blocks_total, 1, per_block)
    half_step = 0.5 * TIME_STEP
    position = positions.reshape(blocks_total, 3, per_block)
    velocity = velocities.reshape(blocks_total, 3, per_block)
    history = [position]
    forces = evaluate(position, None)
    for step_index in range(STEPS):
        midway = velocity + half_step * inverse * forces
        position = position + TIME_STEP * midway
        history.append(position)
        forces = evaluate(position, None)
        velocity = midway + half_step * inverse * forces
    grad_position = pos_cotangent.reshape(blocks_total, 3, per_block)
    grad_velocity = vel_cotangent.reshape(blocks_total, 3, per_block)
    charge_sum = jnp.zeros((blocks_total, per_block), jnp.float32)
    pulled = evaluate(history[STEPS], half_step * inverse * grad_velocity)
    grad_position = grad_position + pulled[:, :3]
    charge_sum = charge_sum + pulled[:, 3]
    for step_index in range(STEPS - 1, -1, -1):
        grad_velocity = grad_velocity + TIME_STEP * grad_position
        factor = TIME_STEP if step_index > 0 else half_step
        pulled = evaluate(history[step_index], factor * inverse * grad_velocity)
        grad_position = grad_position + pulled[:, :3]
        charge_sum = charge_sum + pulled[:, 3]
    grad_charge = charge_sum * alive_mask.reshape(blocks_total, per_block)
    vector_shape = (NX, NY, NZ, 3, per_block)
    return (position.reshape(vector_shape), velocity.reshape(vector_shape), grad_position.reshape(vector_shape), grad_velocity.reshape(vector_shape), grad_charge.reshape(NX, NY, NZ, per_block))
```

```python
import functools
import itertools
import math

import jax
import jax.numpy as jnp
from jax import lax
from jax.experimental import pallas as pl
from jax.experimental.pallas import tpu as pltpu
from jax.sharding import PartitionSpec as P

STEPS = 5
SOFT = 0.04
KAPPA = 2.0
EXPONENT = -KAPPA / math.log(2.0)
TIME_STEP = 0.004
HALF_STEP = 0.5 * TIME_STEP
AXES = ("gx", "gy", "gz")
GROUP = 8
UNROLL = 8
CODES = 64
MESH = pl.DeviceIdType.MESH
VMEM = pl.BlockSpec(memory_space=pltpu.VMEM)
SMEM = pl.BlockSpec(memory_space=pltpu.SMEM)
CUBE = tuple(itertools.product((-1, 0, 1), repeat=3))


class Layout:
    def __init__(self, counts, own, per_block):
        assert own[0] == 1 and own[2] == 1
        self.counts = counts
        self.blocks = own[1]
        self.per_block = per_block
        self.groups = per_block // GROUP
        self.sides = sorted(
            (d for d in CUBE if any(d) and all(c > 1 or not v for c, v in zip(counts, d))),
            key=lambda d: -sum(map(abs, d)),
        )
        self.base = {}
        slot = self.blocks
        for side in self.sides:
            self.base[side] = slot
            slot += self.width(side)
        self.dead = slot
        self.near = [self.neighbours(j) for j in range(self.blocks)]
        self.depth = math.prod(min(3, c * n) for c, n in zip(counts, own)) + 1
        self.most_items = self.blocks * self.groups * (self.depth - 1)

    def width(self, side):
        return 1 if side[1] else self.blocks

    def slot_of(self, x, y, z):
        if 0 <= y < self.blocks:
            side, index = (x, 0, z), y
        else:
            side, index = (x, 1 if y > 0 else -1, z), 0
        if not any(side):
            return index
        return self.base[side] + index if side in self.base else None

    def neighbours(self, j):
        found = []
        for number, d in enumerate(CUBE):
            slot = self.slot_of(d[0], j + d[1], d[2])
            if slot is None:
                continue
            low = tuple(min(v, 0) for v in d)
            lister = self.slot_of(low[0], j + low[1], low[2])
            mine = [-v for v in low]
            other = [v - w for v, w in zip(d, low)]
            code = 0
            for v in mine + other:
                code = 2 * code + v
            found.append((slot, lister, code, number))
        return found


class Peers:
    def __init__(self, layout):
        self.layout = layout
        self.here = tuple(lax.axis_index(axis) for axis in AXES)

    def at(self, side):
        return tuple(place + step for place, step in zip(self.here, side))

    def exists(self, side):
        found = None
        for place, step, count in zip(self.here, side, self.layout.counts):
            if step:
                test = place < count - 1 if step > 0 else place > 0
                found = test if found is None else jnp.logical_and(found, test)
        return found

    def greet(self):
        barrier = pltpu.get_barrier_semaphore()
        for side in self.layout.sides:

            @pl.when(self.exists(side))
            def _(side=side):
                pl.semaphore_signal(barrier, inc=1, device_id=self.at(side), device_id_type=MESH)

        peers = sum(self.exists(side).astype(jnp.int32) for side in self.layout.sides)
        pl.semaphore_wait(barrier, peers)

    def copies(self, source, target, first, send_sem, recv_sem):
        layout = self.layout
        result = []
        for index, side in enumerate(layout.sides):
            back = tuple(-v for v in side)
            wide = layout.width(side)
            start = layout.blocks - 1 if side[1] > 0 else 0
            result.append(
                (
                    self.exists(side),
                    self.exists(back),
                    pltpu.make_async_remote_copy(
                        src_ref=source.at[pl.ds(start, wide)],
                        dst_ref=target.at[pl.ds(layout.base[back] - first, wide)],
                        send_sem=send_sem.at[index],
                        recv_sem=recv_sem.at[index],
                        device_id=self.at(side),
                        device_id_type=MESH,
                    ),
                )
            )
        return result


def start_all(copies):
    for out, unused, copy in copies:

        @pl.when(out)
        def _(copy=copy):
            copy.start()


def wait_all(copies):
    for unused, back, copy in copies:

        @pl.when(back)
        def _(copy=copy):
            copy.wait_recv()

    for out, unused, copy in copies:

        @pl.when(out)
        def _(copy=copy):
            copy.wait_send()


def first_kernel(layout, field_ref, ext_ref, send_sem, recv_sem):
    peers = Peers(layout)
    peers.greet()
    copies = peers.copies(field_ref, ext_ref, 0, send_sem, recv_sem)
    start_all(copies)
    ext_ref[0 : layout.blocks] = field_ref[...]
    ext_ref[layout.dead] = jnp.zeros(ext_ref.shape[1:], jnp.float32)
    for side in layout.sides:

        @pl.when(jnp.logical_not(peers.exists(side)))
        def _(side=side):
            wide = layout.width(side)
            where = pl.ds(layout.base[side], wide)
            ext_ref[where] = jnp.zeros((wide,) + ext_ref.shape[1:], jnp.float32)

    wait_all(copies)


def first_exchange(layout, field):
    sides = len(layout.sides)
    return pl.pallas_call(
        functools.partial(first_kernel, layout),
        out_shape=jax.ShapeDtypeStruct((layout.dead + 1,) + field.shape[1:], jnp.float32),
        in_specs=[VMEM],
        out_specs=VMEM,
        scratch_shapes=[pltpu.SemaphoreType.DMA((sides,)), pltpu.SemaphoreType.DMA((sides,))],
        compiler_params=pltpu.CompilerParams(
            collective_id=1, has_side_effects=True, vmem_limit_bytes=4 * 1024 * 1024
        ),
    )(field)


def table_kernel(layout, info_ref, near_ref, item_ref, last_ref, count_ref, end_ref):
    depth, groups, lanes = layout.depth, layout.groups, layout.per_block
    item = jnp.int32(0)
    for j in range(layout.blocks):
        k = jnp.int32(0)
        offset = jnp.int32(0)
        tiles = jnp.int32(0)
        for slot, lister, code, number in layout.near[j]:
            live = info_ref[lister, 1, code]
            end = offset + live * info_ref[slot, 0, 0]
            cross = (end >= lanes).astype(jnp.int32)
            near_ref[0, j * depth + k] = slot
            near_ref[1, j * depth + k] = number
            near_ref[2, j * depth + k] = offset
            near_ref[3, j * depth + k] = cross * lanes
            end_ref[tiles] = k
            k = k + live
            tiles = tiles + cross
            offset = end - cross * lanes

        def fill(index, carry, j=j, offset=offset):
            near_ref[0, j * depth + index] = layout.dead
            near_ref[1, j * depth + index] = 0
            near_ref[2, j * depth + index] = offset
            near_ref[3, j * depth + index] = 0
            return carry

        lax.fori_loop(k, depth, fill, 0)
        end_ref[tiles] = k
        tiles = tiles + (offset > 0).astype(jnp.int32)
        rows = (info_ref[j, 0, 0] + GROUP - 1) // GROUP

        def one_group(group, item, j=j, tiles=tiles):
            def one_tile(tile, item):
                item_ref[0, item] = j * groups + group
                item_ref[1, item] = j * depth + end_ref[tile]
                item_ref[2, item] = (tile > 0).astype(jnp.int32)
                return item + 1

            item = lax.fori_loop(0, tiles, one_tile, item)
            last_ref[j * groups + group] = jnp.where(tiles > 0, item, 0)
            return item

        item = lax.fori_loop(0, rows, one_group, item)

        def no_group(group, carry, j=j):
            last_ref[j * groups + group] = 0
            return carry

        lax.fori_loop(rows, groups, no_group, 0)
    count_ref[0] = item

    def pad(index, carry):
        item_ref[0, index] = layout.blocks * groups
        item_ref[1, index] = 0
        item_ref[2, index] = 0
        return carry

    lax.fori_loop(item, item_ref.shape[1], pad, 0)


def tables(layout, info):
    return pl.pallas_call(
        functools.partial(table_kernel, layout),
        out_shape=[
            jax.ShapeDtypeStruct((4, layout.blocks * layout.depth), jnp.int32),
            jax.ShapeDtypeStruct((3, layout.most_items), jnp.int32),
            jax.ShapeDtypeStruct((layout.blocks * layout.groups,), jnp.int32),
            jax.ShapeDtypeStruct((1,), jnp.int32),
        ],
        in_specs=[SMEM],
        out_specs=[SMEM] * 4,
        scratch_shapes=[pltpu.SMEM((layout.depth + 1,), jnp.int32)],
        compiler_params=pltpu.CompilerParams(vmem_limit_bytes=4 * 1024 * 1024),
    )(info)


def pair_terms(place, partner, adjoint):
    d = [place(axis) - partner(axis) for axis in range(3)]
    s = d[0] * d[0] + d[1] * d[1] + d[2] * d[2]
    sigma = place("sigma") + partner("sigma")
    square = sigma * sigma
    inverse = 1.0 / (s + square)
    t = square * inverse
    t3 = t * t * t
    soft = s + SOFT
    r = lax.rsqrt(soft)
    b = jnp.exp2(EXPONENT * (soft * r)) * r
    c = jnp.maximum(1.0 - s, 0.0)
    cc = c * c
    p = c * inverse
    y = c * r
    et = place("depth") * partner("depth") * t3
    below = t3 - 1.0
    twice = t3 + below
    half = 1.0 + 0.5 * r
    k1 = 3.0 + y * half
    charge_b = partner("charge") * b
    qb = place("charge") * charge_b
    g1 = cc * (et * (below + p * twice) + qb * k1)
    if not adjoint:
        return [g1 * d[axis] for axis in range(3)]
    h = p * (p * (7.0 * t3 - 2.0) + 3.0 * twice) + below
    k2 = y * (y * (1.0 + r * (1.5 + 0.75 * r)) + 6.0 * half) + 6.0
    k = -2.0 * c * (2.0 * et * h + qb * k2)
    delta = [place(3 + axis) - partner(3 + axis) for axis in range(3)]
    along = delta[0] * d[0] + delta[1] * d[1] + delta[2] * d[2]
    ka = k * along
    terms = [g1 * delta[axis] + ka * d[axis] for axis in range(3)]
    return terms + [cc * k1 * along * charge_b]


def main_kernel(
    layout,
    trips,
    near_ref,
    item_ref,
    last_ref,
    ext_ref,
    vel_ref,
    mass_ref,
    pos_cot_ref,
    vel_cot_ref,
    pos_out,
    vel_out,
    gpos_out,
    gvel_out,
    charge_out,
    own_ref,
    land_ref,
    work_ref,
    shift_ref,
    par_tile,
    pos_tile,
    cot_tile,
    par_row,
    pos_row,
    cot_row,
    sum_ref,
    send_sem,
    recv_sem,
):
    blocks, depth, groups, lanes = layout.blocks, layout.depth, layout.groups, layout.per_block
    dead_row = blocks * groups
    peers = Peers(layout)
    peers.greet()
    lane = lax.broadcasted_iota(jnp.int32, (4, lanes), 1)
    row4 = lax.broadcasted_iota(jnp.int32, (4, lanes), 0)

    for number, d in enumerate(CUBE):
        value = jnp.zeros((4, lanes), jnp.float32)
        for axis in range(3):
            value = jnp.where(row4 == axis, float(d[axis]), value)
        shift_ref[number] = value

    def spread_rows(value4, write):
        turned = jnp.concatenate([value4, value4], axis=0).T
        for part in range(3):
            write(part, jnp.broadcast_to(turned[:, part : part + 1], (lanes, lanes)))

    def pack(read, write, shifted):
        def one(k, carried):
            result = []
            for j in range(blocks):
                at = j * depth + k
                value = read(near_ref[0, at])
                if shifted:
                    value = value + shift_ref[near_ref[1, at]]
                offset = near_ref[2, at]
                turned = pltpu.roll(value, offset, 1)
                current = jnp.where(lane >= offset, turned, carried[j])
                write(at, current)
                result.append(jnp.where(lane < near_ref[3, at], turned, current))
            return tuple(result)

        lax.fori_loop(0, depth, one, (jnp.zeros((4, lanes), jnp.float32),) * blocks)

    def sweep(step, adjoint):
        wide = 4 if adjoint else 3

        def batch(index, total):
            for sub in range(UNROLL):
                item = index * UNROLL + sub
                group = item_ref[0, item]
                tile = item_ref[1, item]
                keep = item_ref[2, item].astype(jnp.float32)
                names = {"charge": 0, "sigma": 1, "depth": 2}

                def place(part):
                    if part in names:
                        return par_row[group, names[part]]
                    return pos_row[step, group, part] if part < 3 else cot_row[group, part - 3]

                def partner(part):
                    if part in names:
                        at = names[part]
                        return par_tile[tile, at : at + 1, :]
                    if part < 3:
                        return pos_tile[step, tile, part : part + 1, :]
                    return cot_tile[tile, part - 3 : part - 2, :]

                terms = pair_terms(place, partner, adjoint)
                total = tuple(keep * old + new for old, new in zip(total, terms))
                for part in range(wide):
                    sum_ref[item + 1, part] = total[part]
            return total

        zero = jnp.zeros((GROUP, lanes), jnp.float32)
        lax.fori_loop(0, trips // UNROLL, batch, (zero,) * wide)
        which = lax.broadcasted_iota(jnp.int32, (lanes, 8), 1)
        result = []
        for j in range(blocks):
            ends = [last_ref[j * groups + group] for group in range(groups)]
            columns = jnp.zeros((lanes, 8), jnp.float32)
            for part in range(wide):
                gathered = jnp.concatenate([sum_ref[end, part] for end in ends], axis=0)
                summed = jnp.sum(gathered, axis=1, keepdims=True)
                columns = jnp.where(which == part, summed, columns)
            result.append(columns.T)
        return result

    zero_row = jnp.zeros((3, GROUP, lanes), jnp.float32)
    par_row[dead_row] = zero_row
    cot_row[dead_row] = zero_row
    for part in range(4):
        sum_ref[0, part] = jnp.zeros((GROUP, lanes), jnp.float32)
    scale_of = {0: 8.0, 1: 1.0, 2: 24.0}
    for j in range(blocks):

        def write(part, value, j=j):
            value = value * scale_of[part]
            par_row[j * groups : (j + 1) * groups, part] = value.reshape(groups, GROUP, lanes)

        spread_rows(ext_ref[j, 1], write)

    def read(slot):
        return ext_ref[slot, 1]

    def write(at, value):
        par_tile[at] = value

    pack(read, write, False)
    work_ref[...] = ext_ref[:, 0]
    inverse = [1.0 / mass_ref[j : j + 1, :] for j in range(blocks)]
    for j in range(blocks):
        vel_out[j] = vel_ref[j]
        pos_out[j] = ext_ref[j, 0, 0:3]
        gpos_out[j] = pos_cot_ref[j]
        gvel_out[j] = vel_cot_ref[j]
        charge_out[j] = jnp.zeros((1, lanes), jnp.float32)

    def exchange(parity):
        copies = peers.copies(
            own_ref.at[parity],
            land_ref.at[parity],
            blocks,
            send_sem.at[parity],
            recv_sem.at[parity],
        )
        start_all(copies)
        wait_all(copies)
        work_ref[0:blocks] = own_ref[parity]
        work_ref[blocks : layout.dead] = land_ref[parity]

    def read_work(slot):
        return work_ref[slot]

    def forward(step, carry):
        for j in range(blocks):

            def write_row(part, value, j=j):
                pos_row[step, j * groups : (j + 1) * groups, part] = value.reshape(
                    groups, GROUP, lanes
                )

            spread_rows(work_ref[j], write_row)
        pos_row[step, dead_row] = zero_row

        def write_tile(at, value):
            pos_tile[step, at] = value

        pack(read_work, write_tile, True)
        force = sweep(step, False)
        inside = jnp.logical_and(step > 0, step < STEPS)
        factor = jnp.where(inside, TIME_STEP, HALF_STEP)
        parity = lax.rem(step, 2)
        for j in range(blocks):
            velocity = vel_out[j] + factor * inverse[j] * force[j][0:3]
            vel_out[j] = velocity

        @pl.when(step < STEPS)
        def _():
            for j in range(blocks):
                position = pos_out[j] + TIME_STEP * vel_out[j]
                pos_out[j] = position
                own_ref[parity, j, 0:3] = position
                own_ref[parity, j, 3:4] = jnp.zeros((1, lanes), jnp.float32)
            exchange(parity)

        return carry

    lax.fori_loop(0, STEPS + 1, forward, 0)
    work_ref[...] = ext_ref[:, 2]

    def backward(index, carry):
        step = STEPS - index
        for j in range(blocks):

            def write_row(part, value, j=j):
                cot_row[j * groups : (j + 1) * groups, part] = value.reshape(groups, GROUP, lanes)

            spread_rows(work_ref[j], write_row)

        def write_tile(at, value):
            cot_tile[at] = value

        pack(read_work, write_tile, False)
        pulled = sweep(step, True)
        for j in range(blocks):
            gpos_out[j] = gpos_out[j] + pulled[j][0:3]
            charge_out[j] = charge_out[j] + pulled[j][3:4]
        factor = jnp.where(step > 1, TIME_STEP, HALF_STEP)
        parity = lax.rem(index + 1, 2)

        @pl.when(index < STEPS)
        def _():
            for j in range(blocks):
                grad = gvel_out[j] + TIME_STEP * gpos_out[j]
                gvel_out[j] = grad
                own_ref[parity, j, 0:3] = factor * inverse[j] * grad
                own_ref[parity, j, 3:4] = jnp.zeros((1, lanes), jnp.float32)
            exchange(parity)

        return carry

    lax.fori_loop(0, STEPS + 1, backward, 0)
    for j in range(blocks):
        alive = lane[0:1] < ext_ref[j, 0, 3:4].astype(jnp.int32)
        charge_out[j] = jnp.where(alive, 8.0 * charge_out[j], 0.0)


def integrate(layout, trips, identity, operands):
    blocks, depth, groups, lanes = layout.blocks, layout.depth, layout.groups, layout.per_block
    sides = len(layout.sides)
    rows = blocks * groups + 1
    vector = jax.ShapeDtypeStruct((blocks, 3, lanes), jnp.float32)
    return pl.pallas_call(
        functools.partial(main_kernel, layout, trips),
        out_shape=[vector] * 4 + [jax.ShapeDtypeStruct((blocks, 1, lanes), jnp.float32)],
        in_specs=[SMEM] * 3 + [VMEM] * 5,
        out_specs=[VMEM] * 5,
        scratch_shapes=[
            pltpu.VMEM((2, blocks, 4, lanes), jnp.float32),
            pltpu.VMEM((2, layout.dead - blocks, 4, lanes), jnp.float32),
            pltpu.VMEM((layout.dead + 1, 4, lanes), jnp.float32),
            pltpu.VMEM((len(CUBE), 4, lanes), jnp.float32),
            pltpu.VMEM((blocks * depth, 4, lanes), jnp.float32),
            pltpu.VMEM((STEPS + 1, blocks * depth, 4, lanes), jnp.float32),
            pltpu.VMEM((blocks * depth, 4, lanes), jnp.float32),
            pltpu.VMEM((rows, 3, GROUP, lanes), jnp.float32),
            pltpu.VMEM((STEPS + 1, rows, 3, GROUP, lanes), jnp.float32),
            pltpu.VMEM((rows, 3, GROUP, lanes), jnp.float32),
            pltpu.VMEM((trips + 1, 4, GROUP, lanes), jnp.float32),
            pltpu.SemaphoreType.DMA((2, sides)),
            pltpu.SemaphoreType.DMA((2, sides)),
        ],
        compiler_params=pltpu.CompilerParams(
            collective_id=identity, has_side_effects=True, vmem_limit_bytes=52 * 1024 * 1024
        ),
    )(*operands)


def atom_params(charges, atom_types, atom_count, sigma_type, epsilon_type):
    type_total = sigma_type.shape[0]
    alive = lax.broadcasted_iota(jnp.int32, charges.shape, 1) < atom_count[:, None]
    alive = alive.astype(jnp.float32)
    matches = atom_types[:, None, :] == lax.broadcasted_iota(jnp.int32, (type_total, 1), 0)
    matches = matches.astype(jnp.float32)
    sigma = jnp.sum(matches * sigma_type[:, None], axis=1)
    depth = jnp.sum(matches * epsilon_type[:, None], axis=1)
    return charges * alive, 0.5 * sigma, jnp.sqrt(depth) * alive


def live_flags(own, pair_list, pair_count):
    extent_y, extent_z = own[1] + 1, own[2] + 1

    def coords(index):
        return index // (extent_y * extent_z), index // extent_z % extent_y, index % extent_z

    one, two = coords(pair_list[0]), coords(pair_list[1])
    low = [jnp.minimum(u, v) for u, v in zip(one, two)]

    def code(place):
        return 4 * (place[0] - low[0]) + 2 * (place[1] - low[1]) + (place[2] - low[2])

    listed = lax.broadcasted_iota(jnp.int32, one[0].shape, 0) < pair_count
    keys = jnp.concatenate([8 * code(one) + code(two), 8 * code(two) + code(one)])
    keys = jnp.where(jnp.concatenate([listed, listed]), keys + CODES * jnp.concatenate([low[1]] * 2), -1)
    match = keys[:, None] == lax.broadcasted_iota(jnp.int32, (1, own[1] * CODES), 1)
    return jnp.any(match, axis=0).astype(jnp.float32).reshape(own[1], CODES)


def classes(most):
    return [most * part // 32 for part in (8, 10, 12, 14, 16, 20, 24, 32)]


def on_device(
    positions,
    velocities,
    charges,
    atom_types,
    atom_count,
    sigma_type,
    epsilon_type,
    masses,
    pair_list,
    pair_count,
    pos_cotangent,
    vel_cotangent,
):
    own = positions.shape[:3]
    lanes = positions.shape[-1]
    layout = Layout(tuple(lax.axis_size(axis) for axis in AXES), own, lanes)
    blocks = layout.blocks

    def flat(array):
        return array.reshape((blocks,) + array.shape[3:])

    count = flat(atom_count)
    charge, sigma, depth = atom_params(
        flat(charges), flat(atom_types), count, sigma_type, epsilon_type
    )
    flags = live_flags(own, pair_list[0, 0, 0], pair_count[0, 0, 0])
    flags = jnp.pad(flags, ((0, 0), (0, lanes - CODES)))
    mass = flat(masses)
    position, cotangent = flat(positions), flat(vel_cotangent)
    counts = jnp.broadcast_to(count.astype(jnp.float32)[:, None, None], (blocks, 1, lanes))
    last_cot = (HALF_STEP * (1.0 / mass))[:, None, :] * cotangent
    field = jnp.stack(
        [
            jnp.concatenate([position, counts], axis=1),
            jnp.stack([charge, sigma, depth, flags], axis=1),
            jnp.concatenate([last_cot, jnp.zeros((blocks, 1, lanes), jnp.float32)], axis=1),
        ],
        axis=1,
    )
    extended = first_exchange(layout, field)
    info = extended[:, 0:2, 3, 0:CODES].astype(jnp.int32)
    near, items, last, total = tables(layout, info)
    most = lax.pmax(total[0], AXES)
    sizes = classes(layout.most_items)
    which = sum((most > size).astype(jnp.int32) for size in sizes[:-1])
    operands = (near, items, last, extended, flat(velocities), mass, flat(pos_cotangent), cotangent)
    branches = [
        functools.partial(integrate, layout, size, 2 + index) for index, size in enumerate(sizes)
    ]
    out = lax.switch(which, branches, operands)
    shapes = [positions.shape] * 4 + [charges.shape]
    return tuple(value.reshape(shape) for value, shape in zip(out, shapes))


def solution(mesh):
    block = P("gx", "gy", "gz")
    in_specs = (block,) * 5 + (P(), P()) + (block,) * 5
    return jax.shard_map(
        on_device, mesh=mesh, in_specs=in_specs, out_specs=(block,) * 5, check_vma=False
    )
```

```python
import functools
import itertools
import math

import jax
import jax.numpy as jnp
from jax import lax
from jax.experimental import pallas as pl
from jax.experimental.pallas import tpu as pltpu
from jax.sharding import PartitionSpec as P

STEPS = 5
SOFT = 0.04
KAPPA = 2.0
EXPONENT = -KAPPA / math.log(2.0)
TIME_STEP = 0.004
HALF_STEP = 0.5 * TIME_STEP
AXES = ("gx", "gy", "gz")
GROUP = 8
UNROLL = 16
CODES = 64
MESH = pl.DeviceIdType.MESH
VMEM = pl.BlockSpec(memory_space=pltpu.VMEM)
SMEM = pl.BlockSpec(memory_space=pltpu.SMEM)
CUBE = tuple(itertools.product((-1, 0, 1), repeat=3))


class Layout:
    def __init__(self, counts, own, per_block):
        assert own[0] == 1 and own[2] == 1
        self.counts = counts
        self.blocks = own[1]
        self.per_block = per_block
        self.groups = per_block // GROUP
        self.sides = sorted(
            (d for d in CUBE if any(d) and all(c > 1 or not v for c, v in zip(counts, d))),
            key=lambda d: -sum(map(abs, d)),
        )
        self.base = {}
        slot = self.blocks
        for side in self.sides:
            self.base[side] = slot
            slot += self.width(side)
        self.dead = slot
        self.near = [self.neighbours(j) for j in range(self.blocks)]
        self.depth = math.prod(min(3, c * n) for c, n in zip(counts, own)) + 1
        self.most_items = self.blocks * self.groups * (self.depth - 1)
        self.list_size = -(-self.most_items // per_block) * per_block

    def width(self, side):
        return 1 if side[1] else self.blocks

    def slot_of(self, x, y, z):
        if 0 <= y < self.blocks:
            side, index = (x, 0, z), y
        else:
            side, index = (x, 1 if y > 0 else -1, z), 0
        if not any(side):
            return index
        return self.base[side] + index if side in self.base else None

    def neighbours(self, j):
        found = []
        for number, d in enumerate(CUBE):
            slot = self.slot_of(d[0], j + d[1], d[2])
            if slot is None:
                continue
            low = tuple(min(v, 0) for v in d)
            lister = self.slot_of(low[0], j + low[1], low[2])
            mine = [-v for v in low]
            other = [v - w for v, w in zip(d, low)]
            code = 0
            for v in mine + other:
                code = 2 * code + v
            found.append((slot, lister, code, number))
        return found


class Peers:
    def __init__(self, layout):
        self.layout = layout
        self.here = tuple(lax.axis_index(axis) for axis in AXES)
        self.total = math.prod(layout.counts)
        self.me = (self.here[0] * layout.counts[1] + self.here[1]) * layout.counts[2] + self.here[2]

    def at(self, side):
        return tuple(place + step for place, step in zip(self.here, side))

    def numbered(self, number):
        unused, count_y, count_z = self.layout.counts
        return (number // (count_y * count_z), number // count_z % count_y, number % count_z)

    def exists(self, side):
        found = None
        for place, step, count in zip(self.here, side, self.layout.counts):
            if step:
                test = place < count - 1 if step > 0 else place > 0
                found = test if found is None else jnp.logical_and(found, test)
        return found

    def others(self, act):
        def one(number, carry):
            @pl.when(number != self.me)
            def _():
                act(number)

            return carry

        lax.fori_loop(0, self.total, one, 0)

    def greet(self):
        barrier = pltpu.get_barrier_semaphore()
        for side in self.layout.sides:

            @pl.when(self.exists(side))
            def _(side=side):
                pl.semaphore_signal(barrier, inc=1, device_id=self.at(side), device_id_type=MESH)

        peers = sum(self.exists(side).astype(jnp.int32) for side in self.layout.sides)
        pl.semaphore_wait(barrier, peers)

    def greet_all(self):
        barrier = pltpu.get_barrier_semaphore()

        def signal(number):
            pl.semaphore_signal(
                barrier, inc=1, device_id=self.numbered(number), device_id_type=MESH
            )

        self.others(signal)
        pl.semaphore_wait(barrier, self.total - 1)

    def copies(self, source, target, first, send_sem, recv_sem):
        layout = self.layout
        result = []
        for index, side in enumerate(layout.sides):
            back = tuple(-v for v in side)
            wide = layout.width(side)
            start = layout.blocks - 1 if side[1] > 0 else 0
            result.append(
                (
                    self.exists(side),
                    self.exists(back),
                    pltpu.make_async_remote_copy(
                        src_ref=source.at[pl.ds(start, wide)],
                        dst_ref=target.at[pl.ds(layout.base[back] - first, wide)],
                        send_sem=send_sem.at[index],
                        recv_sem=recv_sem.at[index],
                        device_id=self.at(side),
                        device_id_type=MESH,
                    ),
                )
            )
        return result


def start_all(copies):
    for out, unused, copy in copies:

        @pl.when(out)
        def _(copy=copy):
            copy.start()


def wait_all(copies):
    for unused, back, copy in copies:

        @pl.when(back)
        def _(copy=copy):
            copy.wait_recv()

    for out, unused, copy in copies:

        @pl.when(out)
        def _(copy=copy):
            copy.wait_send()


def tables(layout, ext_ref, near_ref, item_ref, keep_ref, last_ref):
    blocks, groups, lanes = layout.blocks, layout.groups, layout.per_block
    shape = (blocks, lanes)
    lane = lax.broadcasted_iota(jnp.int32, shape, 1)
    row = lax.broadcasted_iota(jnp.int32, shape, 0)

    def column(values):
        result = jnp.full(shape, values[0], jnp.int32)
        for j, value in enumerate(values[1:], 1):
            result = jnp.where(row == j, value, result)
        return result

    def rows_of(slots, kind):
        return jnp.concatenate([ext_ref[slot, kind, 3:4, :] for slot in slots], axis=0)

    zero = jnp.zeros(shape, jnp.int32)
    rank, offset, tiles, ends = zero, zero, zero, zero
    slots, numbers, offsets, crossings = zero + layout.dead, zero, zero, zero
    for entries in zip(*layout.near):
        code, number = entries[0][2], entries[0][3]
        flag = rows_of([entry[1] for entry in entries], 1)
        live = jnp.broadcast_to(flag[:, code : code + 1], shape).astype(jnp.int32)
        count = rows_of([entry[0] for entry in entries], 0).astype(jnp.int32)
        end = offset + live * count
        cross = (end >= lanes).astype(jnp.int32)
        here = lane == jnp.where(live > 0, rank, -1)
        slots = jnp.where(here, column([entry[0] for entry in entries]), slots)
        numbers = jnp.where(here, number, numbers)
        offsets = jnp.where(here, offset, offsets)
        crossings = jnp.where(here, cross * lanes, crossings)
        ends = jnp.where(lane == jnp.where(cross > 0, tiles, -1), rank, ends)
        rank = rank + live
        tiles = tiles + cross
        offset = end - cross * lanes
    offsets = jnp.where(lane < rank, offsets, offset)
    part = (offset > 0).astype(jnp.int32)
    ends = jnp.where(lane == jnp.where(part > 0, tiles, -1), rank, ends)
    tiles = tiles + part
    for kind, value in enumerate((slots, numbers, offsets, crossings)):
        near_ref[kind * blocks : (kind + 1) * blocks, :] = value

    full = item_ref.shape[1:]
    which = lax.broadcasted_iota(jnp.int32, full, 0) * lanes + lax.broadcasted_iota(
        jnp.int32, full, 1
    )
    group = jnp.full(full, blocks * groups, jnp.int32)
    tile = jnp.zeros(full, jnp.int32)
    keep = jnp.zeros(full, jnp.float32)
    last = jnp.zeros((1, lanes), jnp.int32)
    start = jnp.zeros((1, lanes), jnp.int32)
    lane_one = lane[0:1]
    for j in range(blocks):
        count = ext_ref[j, 0, 3:4, :].astype(jnp.int32)
        rows = (count + (GROUP - 1)) // GROUP
        depth = tiles[j : j + 1]
        some = jnp.maximum(depth, 1)
        relative = which - start
        inside = jnp.logical_and(relative >= 0, relative < rows * depth)
        quotient = (relative.astype(jnp.float32) + 0.5) / some.astype(jnp.float32)
        index = jnp.floor(quotient).astype(jnp.int32)
        along = relative - index * some
        found = jnp.zeros(full, jnp.int32)
        for number in range(layout.depth):
            value = jnp.broadcast_to(ends[j : j + 1, number : number + 1], (1, lanes))
            found = jnp.where(along == number, value, found)
        group = jnp.where(inside, j * groups + index, group)
        tile = jnp.where(inside, j * layout.depth + found, tile)
        keep = jnp.where(jnp.logical_and(inside, along > 0), 1.0, keep)
        place = lane_one - j * groups
        known = jnp.logical_and(
            jnp.logical_and(place >= 0, place < rows), jnp.logical_and(place < groups, depth > 0)
        )
        last = jnp.where(known, start + (place + 1) * depth, last)
        start = start + rows * depth
    item_ref[0] = group
    item_ref[1] = tile
    keep_ref[...] = keep
    last_ref[...] = last
    return start


def first_kernel(
    layout,
    field_ref,
    ext_ref,
    near_ref,
    item_ref,
    keep_ref,
    last_ref,
    most_ref,
    own_ref,
    all_ref,
    send_sem,
    recv_sem,
    send_all,
    recv_all,
):
    peers = Peers(layout)
    peers.greet_all()
    copies = peers.copies(field_ref, ext_ref, 0, send_sem, recv_sem)
    start_all(copies)
    ext_ref[0 : layout.blocks] = field_ref[...]
    ext_ref[layout.dead] = jnp.zeros(ext_ref.shape[1:], jnp.float32)
    for side in layout.sides:

        @pl.when(jnp.logical_not(peers.exists(side)))
        def _(side=side):
            wide = layout.width(side)
            where = pl.ds(layout.base[side], wide)
            ext_ref[where] = jnp.zeros((wide,) + ext_ref.shape[1:], jnp.float32)

    wait_all(copies)
    total = tables(layout, ext_ref, near_ref, item_ref, keep_ref, last_ref)
    own_ref[0] = total.astype(jnp.float32)

    def moved(index, target):
        return pltpu.make_async_remote_copy(
            src_ref=own_ref,
            dst_ref=all_ref.at[pl.ds(index, 1)],
            send_sem=send_all.at[target],
            recv_sem=recv_all.at[index],
            device_id=peers.numbered(target),
            device_id_type=MESH,
        )

    peers.others(lambda number: moved(peers.me, number).start())
    all_ref[pl.ds(peers.me, 1)] = own_ref[...]
    peers.others(lambda number: moved(number, number).wait_recv())
    peers.others(lambda number: moved(number, number).wait_send())
    most_ref[...] = jnp.max(all_ref[...], axis=0).astype(jnp.int32)


def first_exchange(layout, field):
    sides = len(layout.sides)
    lanes = layout.per_block
    total = math.prod(layout.counts)
    height = -(-layout.most_items // lanes)
    return pl.pallas_call(
        functools.partial(first_kernel, layout),
        out_shape=[
            jax.ShapeDtypeStruct((layout.dead + 1,) + field.shape[1:], jnp.float32),
            jax.ShapeDtypeStruct((4 * layout.blocks, lanes), jnp.int32),
            jax.ShapeDtypeStruct((2, height, lanes), jnp.int32),
            jax.ShapeDtypeStruct((height, lanes), jnp.float32),
            jax.ShapeDtypeStruct((1, lanes), jnp.int32),
            jax.ShapeDtypeStruct((1, lanes), jnp.int32),
        ],
        in_specs=[VMEM],
        out_specs=[VMEM] * 6,
        scratch_shapes=[
            pltpu.VMEM((1, 1, lanes), jnp.float32),
            pltpu.VMEM((total, 1, lanes), jnp.float32),
            pltpu.SemaphoreType.DMA((sides,)),
            pltpu.SemaphoreType.DMA((sides,)),
            pltpu.SemaphoreType.DMA((total,)),
            pltpu.SemaphoreType.DMA((total,)),
        ],
        compiler_params=pltpu.CompilerParams(
            collective_id=1, has_side_effects=True, vmem_limit_bytes=4 * 1024 * 1024
        ),
    )(field)


def pair_terms(place, partner, force, adjoint):
    d = [place("position", axis) - partner("position", axis) for axis in range(3)]
    s = d[0] * d[0] + d[1] * d[1] + d[2] * d[2]
    sigma = place("sigma") + partner("sigma")
    square = sigma * sigma
    inverse = 1.0 / (s + square)
    t = square * inverse
    t3 = t * t * t
    soft = s + SOFT
    r = lax.rsqrt(soft)
    b = jnp.exp2(EXPONENT * (soft * r)) * r
    c = jnp.maximum(1.0 - s, 0.0)
    cc = c * c
    p = c * inverse
    y = c * r
    et = place("depth") * partner("depth") * t3
    below = t3 - 1.0
    twice = t3 + below
    half = 1.0 + 0.5 * r
    k1 = 3.0 + y * half
    charge_b = partner("charge") * b
    qb = place("charge") * charge_b
    g1 = cc * (et * (below + p * twice) + qb * k1)
    terms = [g1 * d[axis] for axis in range(3)] if force else []
    if not adjoint:
        return terms, []
    h = p * (p * (7.0 * t3 - 2.0) + 3.0 * twice) + below
    k2 = y * (y * (1.0 + r * (1.5 + 0.75 * r)) + 6.0 * half) + 6.0
    k = -2.0 * c * (2.0 * et * h + qb * k2)
    return terms, [g1, k, cc * k1 * charge_b]


def pulled_terms(place, partner, g1, k, m):
    d = [place("position", axis) - partner("position", axis) for axis in range(3)]
    delta = [place("cotangent", axis) - partner("cotangent", axis) for axis in range(3)]
    along = delta[0] * d[0] + delta[1] * d[1] + delta[2] * d[2]
    ka = k * along
    return [g1 * delta[axis] + ka * d[axis] for axis in range(3)] + [m * along]


ROW_AT = {"charge": 0, "sigma": 1, "depth": 2, "position": 3, "cotangent": 6}
TILE_AT = {"charge": 0, "sigma": 1, "depth": 2, "position": 4, "cotangent": 8}


def main_kernel(
    layout,
    trips,
    near_ref,
    item_ref,
    keep_ref,
    last_ref,
    ext_ref,
    vel_ref,
    mass_ref,
    pos_cot_ref,
    vel_cot_ref,
    pos_out,
    vel_out,
    gpos_out,
    gvel_out,
    charge_out,
    own_ref,
    land_ref,
    work_ref,
    shift_ref,
    place_ref,
    past_ref,
    tile_ref,
    row_ref,
    sum_ref,
    send_sem,
    recv_sem,
):
    blocks, depth, groups, lanes = layout.blocks, layout.depth, layout.groups, layout.per_block
    tiles = blocks * depth
    dead_row = blocks * groups
    peers = Peers(layout)
    lane = lax.broadcasted_iota(jnp.int32, (4, lanes), 1)
    row4 = lax.broadcasted_iota(jnp.int32, (4, lanes), 0)

    for number, d in enumerate(CUBE):
        value = jnp.zeros((4, lanes), jnp.float32)
        for axis in range(3):
            value = jnp.where(row4 == axis, float(d[axis]), value)
        shift_ref[number] = value

    def spread_rows(first, values, scales=(1.0, 1.0, 1.0)):
        for j, value in enumerate(values):
            turned = jnp.concatenate([value, value], axis=0).T
            for part in range(3):
                wide = jnp.broadcast_to(turned[:, part : part + 1], (lanes, lanes))
                if scales[part] != 1.0:
                    wide = wide * scales[part]
                row_ref[j * groups : (j + 1) * groups, first + part] = wide.reshape(
                    groups, GROUP, lanes
                )

    def pack(read, first, shifted):
        carried = [jnp.zeros((4, lanes), jnp.float32)] * blocks
        for k in range(depth):
            for j in range(blocks):
                value = read(near_ref[j, k])
                if shifted:
                    value = value + shift_ref[near_ref[blocks + j, k]]
                offset = near_ref[2 * blocks + j, k]
                turned = pltpu.roll(value, offset, 1)
                current = jnp.where(lane >= offset, turned, carried[j])
                tile_ref[j * depth + k, first : first + 4, :] = current
                carried[j] = jnp.where(lane < near_ref[3 * blocks + j, k], turned, current)

    def access(item):
        group = item_ref[item]
        tile = item_ref[layout.list_size + item]

        def place(name, axis=0):
            return row_ref[group, ROW_AT[name] + axis]

        def partner(name, axis=0):
            at = TILE_AT[name] + axis
            return tile_ref[tile, at : at + 1, :]

        return place, partner

    def run(body, wide):
        def batch(index, total):
            base = index * UNROLL
            found = [body(base + sub) for sub in range(UNROLL)]
            for sub in range(UNROLL):
                item = base + sub
                sums, kept = found[sub]
                for part, value in enumerate(kept):
                    sum_ref[item + 1, 3 + part] = value
                keep = keep_ref[item]
                total = tuple(keep * old + new for old, new in zip(total, sums))
                for part, value in enumerate(total):
                    sum_ref[item + 1, part] = value
            return total

        zero = jnp.zeros((GROUP, lanes), jnp.float32)
        lax.fori_loop(0, trips // UNROLL, batch, (zero,) * wide)

    def reduced(wide):
        which = lax.broadcasted_iota(jnp.int32, (lanes, 8), 1)
        result = []
        for j in range(blocks):
            ends = [last_ref[0, j * groups + group] for group in range(groups)]
            columns = jnp.zeros((lanes, 8), jnp.float32)
            for part in range(wide):
                gathered = jnp.concatenate([sum_ref[end, part] for end in ends], axis=0)
                summed = jnp.sum(gathered, axis=1, keepdims=True)
                columns = jnp.where(which == part, summed, columns)
            result.append(columns.T)
        return result

    def force_item(item):
        return pair_terms(*access(item), True, False)

    def both_item(item):
        return pair_terms(*access(item), True, True)

    def coefficient_item(item):
        return pair_terms(*access(item), False, True)

    def pulled_item(item):
        coefficients = [sum_ref[item + 1, 3 + part] for part in range(3)]
        return pulled_terms(*access(item), *coefficients), []

    def read_work(slot):
        return work_ref[slot]

    def arrived(parity):
        work_ref[0:blocks] = own_ref[parity]
        work_ref[blocks : layout.dead] = land_ref[parity]

    def copies_of(parity):
        return peers.copies(
            own_ref.at[parity],
            land_ref.at[parity],
            blocks,
            send_sem.at[parity],
            recv_sem.at[parity],
        )

    zero_four = jnp.zeros((1, lanes), jnp.float32)
    row_ref[dead_row] = jnp.zeros(row_ref.shape[1:], jnp.float32)
    for part in range(sum_ref.shape[1]):
        sum_ref[0, part] = jnp.zeros((GROUP, lanes), jnp.float32)
    spread_rows(ROW_AT["charge"], [ext_ref[j, 1] for j in range(blocks)], (8.0, 1.0, 24.0))
    pack(lambda slot: ext_ref[slot, 1], TILE_AT["charge"], False)
    work_ref[...] = ext_ref[:, 0]
    inverse = [1.0 / mass_ref[j : j + 1, :] for j in range(blocks)]
    for j in range(blocks):
        vel_out[j] = vel_ref[j]
        pos_out[j] = ext_ref[j, 0, 0:3]
        place_ref[0, j] = ext_ref[j, 0]
        gpos_out[j] = pos_cot_ref[j]
        gvel_out[j] = vel_cot_ref[j]
        charge_out[j] = jnp.zeros((1, lanes), jnp.float32)
    spread_rows(ROW_AT["position"], [work_ref[j] for j in range(blocks)])
    at_position = pl.ds(TILE_AT["position"], 4)
    peers.greet()

    def forward(step, carry):
        pack(read_work, TILE_AT["position"], True)
        for tile in range(tiles):
            past_ref[step, tile] = tile_ref[tile, at_position, :]
        run(force_item, 3)
        force = reduced(3)
        factor = jnp.where(step > 0, TIME_STEP, HALF_STEP)
        parity = lax.rem(step, 2)
        for j in range(blocks):
            velocity = vel_out[j] + factor * inverse[j] * force[j][0:3]
            vel_out[j] = velocity
            position = pos_out[j] + TIME_STEP * velocity
            pos_out[j] = position
            own_ref[parity, j] = jnp.concatenate([position, zero_four], axis=0)
        copies = copies_of(parity)
        start_all(copies)
        for j in range(blocks):
            place_ref[step + 1, j] = own_ref[parity, j]
        spread_rows(ROW_AT["position"], [own_ref[parity, j] for j in range(blocks)])
        wait_all(copies)
        arrived(parity)
        return carry

    lax.fori_loop(0, STEPS, forward, 0)
    pack(read_work, TILE_AT["position"], True)
    run(both_item, 3)
    force = reduced(3)
    for j in range(blocks):
        vel_out[j] = vel_out[j] + HALF_STEP * inverse[j] * force[j][0:3]
    work_ref[...] = ext_ref[:, 2]
    spread_rows(ROW_AT["cotangent"], [work_ref[j] for j in range(blocks)])

    def backward(index, carry):
        step = STEPS - index
        pack(read_work, TILE_AT["cotangent"], False)
        run(pulled_item, 4)
        pulled = reduced(4)
        for j in range(blocks):
            gpos_out[j] = gpos_out[j] + pulled[j][0:3]
            charge_out[j] = charge_out[j] + pulled[j][3:4]

        @pl.when(index < STEPS)
        def _():
            factor = jnp.where(step > 1, TIME_STEP, HALF_STEP)
            parity = lax.rem(index + STEPS, 2)
            for j in range(blocks):
                grad = gvel_out[j] + TIME_STEP * gpos_out[j]
                gvel_out[j] = grad
                own_ref[parity, j] = jnp.concatenate(
                    [factor * inverse[j] * grad, zero_four], axis=0
                )
            copies = copies_of(parity)
            start_all(copies)
            spread_rows(ROW_AT["cotangent"], [own_ref[parity, j] for j in range(blocks)])
            spread_rows(ROW_AT["position"], [place_ref[step - 1, j] for j in range(blocks)])
            for tile in range(tiles):
                tile_ref[tile, at_position, :] = past_ref[step - 1, tile]
            run(coefficient_item, 0)
            wait_all(copies)
            arrived(parity)

        return carry

    lax.fori_loop(0, STEPS + 1, backward, 0)
    for j in range(blocks):
        alive = lane[0:1] < ext_ref[j, 0, 3:4].astype(jnp.int32)
        charge_out[j] = jnp.where(alive, 8.0 * charge_out[j], 0.0)


def integrate(layout, trips, identity, operands):
    blocks, depth, groups, lanes = layout.blocks, layout.depth, layout.groups, layout.per_block
    sides = len(layout.sides)
    rows = blocks * groups + 1
    vector = jax.ShapeDtypeStruct((blocks, 3, lanes), jnp.float32)
    return pl.pallas_call(
        functools.partial(main_kernel, layout, trips),
        out_shape=[vector] * 4 + [jax.ShapeDtypeStruct((blocks, 1, lanes), jnp.float32)],
        in_specs=[SMEM] * 4 + [VMEM] * 5,
        out_specs=[VMEM] * 5,
        scratch_shapes=[
            pltpu.VMEM((2, blocks, 4, lanes), jnp.float32),
            pltpu.VMEM((2, layout.dead - blocks, 4, lanes), jnp.float32),
            pltpu.VMEM((layout.dead + 1, 4, lanes), jnp.float32),
            pltpu.VMEM((len(CUBE), 4, lanes), jnp.float32),
            pltpu.VMEM((STEPS + 1, blocks, 4, lanes), jnp.float32),
            pltpu.VMEM((STEPS, blocks * depth, 4, lanes), jnp.float32),
            pltpu.VMEM((blocks * depth, 16, lanes), jnp.float32),
            pltpu.VMEM((rows, 9, GROUP, lanes), jnp.float32),
            pltpu.VMEM((trips + 1, 6, GROUP, lanes), jnp.float32),
            pltpu.SemaphoreType.DMA((2, sides)),
            pltpu.SemaphoreType.DMA((2, sides)),
        ],
        compiler_params=pltpu.CompilerParams(
            collective_id=identity, has_side_effects=True, vmem_limit_bytes=52 * 1024 * 1024
        ),
    )(*operands)


def atom_params(charges, atom_types, atom_count, sigma_type, epsilon_type):
    type_total = sigma_type.shape[0]
    alive = lax.broadcasted_iota(jnp.int32, charges.shape, 1) < atom_count[:, None]
    alive = alive.astype(jnp.float32)
    matches = atom_types[:, None, :] == lax.broadcasted_iota(jnp.int32, (type_total, 1), 0)
    matches = matches.astype(jnp.float32)
    sigma = jnp.sum(matches * sigma_type[:, None], axis=1)
    depth = jnp.sum(matches * epsilon_type[:, None], axis=1)
    return charges * alive, 0.5 * sigma, jnp.sqrt(depth) * alive


def live_flags(own, pair_list, pair_count):
    extent_y, extent_z = own[1] + 1, own[2] + 1

    def coords(index):
        return index // (extent_y * extent_z), index // extent_z % extent_y, index % extent_z

    one, two = coords(pair_list[0]), coords(pair_list[1])
    low = [jnp.minimum(u, v) for u, v in zip(one, two)]

    def code(place):
        return 4 * (place[0] - low[0]) + 2 * (place[1] - low[1]) + (place[2] - low[2])

    listed = lax.broadcasted_iota(jnp.int32, one[0].shape, 0) < pair_count
    keys = jnp.concatenate([8 * code(one) + code(two), 8 * code(two) + code(one)])
    keys = jnp.where(jnp.concatenate([listed, listed]), keys + CODES * jnp.concatenate([low[1]] * 2), -1)
    match = keys[:, None] == lax.broadcasted_iota(jnp.int32, (1, own[1] * CODES), 1)
    return jnp.any(match, axis=0).astype(jnp.float32).reshape(own[1], CODES)


def classes(most):
    return [-(-most * part // 32 // UNROLL) * UNROLL for part in (10, 12, 13, 14, 16, 20, 32)]


def on_device(
    positions,
    velocities,
    charges,
    atom_types,
    atom_count,
    sigma_type,
    epsilon_type,
    masses,
    pair_list,
    pair_count,
    pos_cotangent,
    vel_cotangent,
):
    own = positions.shape[:3]
    lanes = positions.shape[-1]
    layout = Layout(tuple(lax.axis_size(axis) for axis in AXES), own, lanes)
    blocks = layout.blocks

    def flat(array):
        return array.reshape((blocks,) + array.shape[3:])

    count = flat(atom_count)
    charge, sigma, depth = atom_params(
        flat(charges), flat(atom_types), count, sigma_type, epsilon_type
    )
    flags = live_flags(own, pair_list[0, 0, 0], pair_count[0, 0, 0])
    flags = jnp.pad(flags, ((0, 0), (0, lanes - CODES)))
    mass = flat(masses)
    position, cotangent = flat(positions), flat(vel_cotangent)
    counts = jnp.broadcast_to(count.astype(jnp.float32)[:, None, None], (blocks, 1, lanes))
    last_cot = (HALF_STEP * (1.0 / mass))[:, None, :] * cotangent
    field = jnp.stack(
        [
            jnp.concatenate([position, counts], axis=1),
            jnp.stack([charge, sigma, depth, flags], axis=1),
            jnp.concatenate([last_cot, jnp.zeros((blocks, 1, lanes), jnp.float32)], axis=1),
        ],
        axis=1,
    )
    extended, near, items, keep, last, most = first_exchange(layout, field)
    items, keep, most = items.reshape(-1), keep.reshape(-1), most[0, 0]
    sizes = classes(layout.most_items)
    which = sum((most > size).astype(jnp.int32) for size in sizes[:-1])
    operands = (near, items, keep, last, extended, flat(velocities), mass, flat(pos_cotangent), cotangent)
    branches = [
        functools.partial(integrate, layout, size, 2 + index) for index, size in enumerate(sizes)
    ]
    out = lax.switch(which, branches, operands)
    shapes = [positions.shape] * 4 + [charges.shape]
    return tuple(value.reshape(shape) for value, shape in zip(out, shapes))


def solution(mesh):
    block = P("gx", "gy", "gz")
    in_specs = (block,) * 5 + (P(), P()) + (block,) * 5
    return jax.shard_map(
        on_device, mesh=mesh, in_specs=in_specs, out_specs=(block,) * 5, check_vma=False
    )
```

```python
import functools
import itertools
import math

import jax
import jax.numpy as jnp
from jax import lax
from jax.experimental import pallas as pl
from jax.experimental.pallas import tpu as pltpu
from jax.sharding import PartitionSpec as P

STEPS = 5
SOFT = 0.04
KAPPA = 2.0
EXPONENT = -KAPPA / math.log(2.0)
TIME_STEP = 0.004
HALF_STEP = 0.5 * TIME_STEP
AXES = ("gx", "gy", "gz")
GROUP = 8
UNROLL = 24
VMEM_FIRST = 32 * 1024 * 1024
MESH = pl.DeviceIdType.MESH
VMEM = pl.BlockSpec(memory_space=pltpu.VMEM)
SMEM = pl.BlockSpec(memory_space=pltpu.SMEM)
CUBE = tuple(itertools.product((-1, 0, 1), repeat=3))


class Layout:
    def __init__(self, counts, own, per_block):
        assert own[0] == 1 and own[2] == 1
        self.counts = counts
        self.blocks = own[1]
        self.per_block = per_block
        self.groups = per_block // GROUP
        self.sides = sorted(
            (d for d in CUBE if any(d) and all(c > 1 or not v for c, v in zip(counts, d))),
            key=lambda d: -sum(map(abs, d)),
        )
        self.base = {}
        slot = self.blocks
        for side in self.sides:
            self.base[side] = slot
            slot += self.width(side)
        self.dead = slot
        self.near = [self.neighbours(j) for j in range(self.blocks)]
        self.depth = math.prod(min(3, c * n) for c, n in zip(counts, own)) + 1
        self.most_items = self.blocks * self.groups * (self.depth - 1)
        self.list_size = -(-self.most_items // per_block) * per_block

    def width(self, side):
        return 1 if side[1] else self.blocks

    def slot_of(self, x, y, z):
        if 0 <= y < self.blocks:
            side, index = (x, 0, z), y
        else:
            side, index = (x, 1 if y > 0 else -1, z), 0
        if not any(side):
            return index
        return self.base[side] + index if side in self.base else None

    def neighbours(self, j):
        found = []
        for number, d in enumerate(CUBE):
            slot = self.slot_of(d[0], j + d[1], d[2])
            if slot is None:
                continue
            low = tuple(min(v, 0) for v in d)
            lister = self.slot_of(low[0], j + low[1], low[2])
            mine = [-v for v in low]
            other = [v - w for v, w in zip(d, low)]
            code = 0
            for v in mine + other:
                code = 2 * code + v
            found.append((slot, lister, code, number))
        return found


class Peers:
    def __init__(self, layout):
        self.layout = layout
        self.here = tuple(lax.axis_index(axis) for axis in AXES)
        self.total = math.prod(layout.counts)
        self.me = (self.here[0] * layout.counts[1] + self.here[1]) * layout.counts[2] + self.here[2]

    def at(self, side):
        return tuple(place + step for place, step in zip(self.here, side))

    def numbered(self, number):
        unused, count_y, count_z = self.layout.counts
        return (number // (count_y * count_z), number // count_z % count_y, number % count_z)

    def exists(self, side):
        found = None
        for place, step, count in zip(self.here, side, self.layout.counts):
            if step:
                test = place < count - 1 if step > 0 else place > 0
                found = test if found is None else jnp.logical_and(found, test)
        return found

    def others(self, act):
        def one(number, carry):
            @pl.when(number != self.me)
            def _():
                act(number)

            return carry

        lax.fori_loop(0, self.total, one, 0)

    def greet(self):
        barrier = pltpu.get_barrier_semaphore()
        for side in self.layout.sides:

            @pl.when(self.exists(side))
            def _(side=side):
                pl.semaphore_signal(barrier, inc=1, device_id=self.at(side), device_id_type=MESH)

        peers = sum(self.exists(side).astype(jnp.int32) for side in self.layout.sides)
        pl.semaphore_wait(barrier, peers)

    def greet_all(self):
        barrier = pltpu.get_barrier_semaphore()

        def signal(number):
            pl.semaphore_signal(
                barrier, inc=1, device_id=self.numbered(number), device_id_type=MESH
            )

        self.others(signal)
        return lambda: pl.semaphore_wait(barrier, self.total - 1)

    def copies(self, source, target, first, send_sem, recv_sem):
        layout = self.layout
        result = []
        for index, side in enumerate(layout.sides):
            back = tuple(-v for v in side)
            wide = layout.width(side)
            start = layout.blocks - 1 if side[1] > 0 else 0
            result.append(
                (
                    self.exists(side),
                    self.exists(back),
                    pltpu.make_async_remote_copy(
                        src_ref=source.at[pl.ds(start, wide)],
                        dst_ref=target.at[pl.ds(layout.base[back] - first, wide)],
                        send_sem=send_sem.at[index],
                        recv_sem=recv_sem.at[index],
                        device_id=self.at(side),
                        device_id_type=MESH,
                    ),
                )
            )
        return result


def start_all(copies):
    for out, unused, copy in copies:

        @pl.when(out)
        def _(copy=copy):
            copy.start()


def wait_all(copies):
    for unused, back, copy in copies:

        @pl.when(back)
        def _(copy=copy):
            copy.wait_recv()

    for out, unused, copy in copies:

        @pl.when(out)
        def _(copy=copy):
            copy.wait_send()


def tables(layout, ext_ref, near_ref, item_ref, keep_ref, last_ref):
    blocks, groups, lanes = layout.blocks, layout.groups, layout.per_block
    shape = (blocks, lanes)
    lane = lax.broadcasted_iota(jnp.int32, shape, 1)
    row = lax.broadcasted_iota(jnp.int32, shape, 0)

    def column(values):
        result = jnp.full(shape, values[0], jnp.int32)
        for j, value in enumerate(values[1:], 1):
            result = jnp.where(row == j, value, result)
        return result

    def rows_of(slots, kind):
        return jnp.concatenate([ext_ref[slot, kind, 3:4, :] for slot in slots], axis=0)

    zero = jnp.zeros(shape, jnp.int32)
    rank, offset, tiles, ends = zero, zero, zero, zero
    slots, numbers, offsets, crossings = zero + layout.dead, zero, zero, zero
    for entries in zip(*layout.near):
        code, number = entries[0][2], entries[0][3]
        flag = rows_of([entry[1] for entry in entries], 1)
        live = jnp.broadcast_to(flag[:, code : code + 1], shape).astype(jnp.int32)
        count = rows_of([entry[0] for entry in entries], 0).astype(jnp.int32)
        end = offset + live * count
        cross = (end >= lanes).astype(jnp.int32)
        here = lane == jnp.where(live > 0, rank, -1)
        slots = jnp.where(here, column([entry[0] for entry in entries]), slots)
        numbers = jnp.where(here, number, numbers)
        offsets = jnp.where(here, offset, offsets)
        crossings = jnp.where(here, cross * lanes, crossings)
        ends = jnp.where(lane == jnp.where(cross > 0, tiles, -1), rank, ends)
        rank = rank + live
        tiles = tiles + cross
        offset = end - cross * lanes
    offsets = jnp.where(lane < rank, offsets, offset)
    part = (offset > 0).astype(jnp.int32)
    ends = jnp.where(lane == jnp.where(part > 0, tiles, -1), rank, ends)
    tiles = tiles + part
    for kind, value in enumerate((slots, numbers, offsets, crossings)):
        near_ref[kind * blocks : (kind + 1) * blocks, :] = value

    heights = [(ext_ref[j, 0, 3:4, :].astype(jnp.int32) + (GROUP - 1)) // GROUP for j in range(blocks)]
    total = sum(heights[j] * tiles[j : j + 1] for j in range(blocks))

    def write_list():
        full = item_ref.shape[1:]
        which = lax.broadcasted_iota(jnp.int32, full, 0) * lanes + lax.broadcasted_iota(
            jnp.int32, full, 1
        )
        group = jnp.full(full, blocks * groups, jnp.int32)
        tile = jnp.zeros(full, jnp.int32)
        keep = jnp.zeros(full, jnp.float32)
        last = jnp.zeros((1, lanes), jnp.int32)
        start = jnp.zeros((1, lanes), jnp.int32)
        lane_one = lane[0:1]
        for j in range(blocks):
            rows = heights[j]
            depth = tiles[j : j + 1]
            some = jnp.maximum(depth, 1)
            relative = which - start
            inside = jnp.logical_and(relative >= 0, relative < rows * depth)
            quotient = (relative.astype(jnp.float32) + 0.5) / some.astype(jnp.float32)
            index = jnp.floor(quotient).astype(jnp.int32)
            along = relative - index * some
            found = jnp.zeros(full, jnp.int32)
            for number in range(layout.depth):
                value = jnp.broadcast_to(ends[j : j + 1, number : number + 1], (1, lanes))
                found = jnp.where(along == number, value, found)
            group = jnp.where(inside, j * groups + index, group)
            tile = jnp.where(inside, j * layout.depth + found, tile)
            keep = jnp.where(jnp.logical_and(inside, along > 0), 1.0, keep)
            place = lane_one - j * groups
            known = jnp.logical_and(
                jnp.logical_and(place >= 0, place < rows), jnp.logical_and(place < groups, depth > 0)
            )
            last = jnp.where(known, start + (place + 1) * depth, last)
            start = start + rows * depth
        item_ref[0] = group
        item_ref[1] = tile
        keep_ref[...] = keep
        last_ref[...] = last

    return total, write_list


def vector_rows(ref, j):
    return jnp.concatenate([ref[j, axis] for axis in range(3)], axis=0)


def divided(value, divisor):
    return (value * (65536 // divisor + 1)) >> 16


def live_flags(layout, pair_ref, count_ref, shape):
    row = lax.broadcasted_iota(jnp.int32, shape, 0)
    lane = lax.broadcasted_iota(jnp.int32, shape, 1)
    extent_y, extent_z = layout.blocks + 1, 2

    def coords(index):
        x = divided(index, extent_y * extent_z)
        index = index - x * (extent_y * extent_z)
        y = divided(index, extent_z)
        return x, y, index - y * extent_z

    def one(slot, flags):
        one, two = coords(pair_ref[0, slot]), coords(pair_ref[1, slot])
        low = [jnp.minimum(u, v) for u, v in zip(one, two)]

        def code(place):
            return 4 * (place[0] - low[0]) + 2 * (place[1] - low[1]) + (place[2] - low[2])

        first, second = code(one), code(two)
        here = jnp.logical_or(lane == 8 * first + second, lane == 8 * second + first)
        here = jnp.logical_and(here, row == low[1])
        here = jnp.logical_and(here, jnp.zeros(shape, jnp.int32) + slot < count_ref[0])
        return jnp.where(here, 1.0, flags)

    return lax.fori_loop(0, pair_ref.shape[1], one, jnp.zeros(shape, jnp.float32))


def first_kernel(
    layout,
    pos_hbm,
    cot_hbm,
    mass_hbm,
    charge_hbm,
    type_hbm,
    number_ref,
    sigma_ref,
    epsilon_ref,
    pair_ref,
    live_ref,
    ext_ref,
    near_ref,
    item_ref,
    keep_ref,
    last_ref,
    most_ref,
    pos_ref,
    cot_ref,
    mass_ref,
    charge_ref,
    type_ref,
    field_ref,
    own_ref,
    all_ref,
    load_sem,
    send_sem,
    recv_sem,
    send_all,
    recv_all,
):
    blocks = layout.blocks
    shape = (blocks, layout.per_block)
    peers = Peers(layout)
    met = peers.greet_all()
    loads = [
        pltpu.make_async_copy(source, target, load_sem.at[index])
        for index, (source, target) in enumerate(
            zip(
                (pos_hbm, cot_hbm, mass_hbm, charge_hbm, type_hbm),
                (pos_ref, cot_ref, mass_ref, charge_ref, type_ref),
            )
        )
    ]
    for load in loads:
        load.start()
    flags = live_flags(layout, pair_ref, live_ref, shape)
    row = lax.broadcasted_iota(jnp.int32, shape, 0)
    count = jnp.zeros(shape, jnp.int32)
    for j in range(blocks):
        count = jnp.where(row == j, number_ref[j], count)
    alive = (lax.broadcasted_iota(jnp.int32, shape, 1) < count).astype(jnp.float32)
    ext_ref[layout.dead] = jnp.zeros(ext_ref.shape[1:], jnp.float32)
    for side in layout.sides:

        @pl.when(jnp.logical_not(peers.exists(side)))
        def _(side=side):
            wide = layout.width(side)
            where = pl.ds(layout.base[side], wide)
            ext_ref[where] = jnp.zeros((wide,) + ext_ref.shape[1:], jnp.float32)

    for load in loads:
        load.wait()
    types = type_ref[...]
    sigma = jnp.zeros(shape, jnp.float32)
    depth = jnp.zeros(shape, jnp.float32)
    for kind in range(sigma_ref.shape[0]):
        sigma = jnp.where(types == kind, 0.5 * sigma_ref[kind], sigma)
        depth = jnp.where(types == kind, epsilon_ref[kind], depth)
    rows = (charge_ref[...] * alive, sigma, jnp.sqrt(depth) * alive, flags)
    scale = HALF_STEP * (1.0 / mass_ref[...])
    number = count.astype(jnp.float32)
    for j in range(blocks):
        own = slice(j, j + 1)
        field_ref[j, 0] = jnp.concatenate([vector_rows(pos_ref, j), number[own]], axis=0)
        field_ref[j, 1] = jnp.concatenate([value[own] for value in rows], axis=0)
        field_ref[j, 2] = jnp.concatenate(
            [scale[own] * vector_rows(cot_ref, j), jnp.zeros_like(number[own])], axis=0
        )
    met()
    copies = peers.copies(field_ref, ext_ref, 0, send_sem, recv_sem)
    start_all(copies)
    ext_ref[0:blocks] = field_ref[...]
    wait_all(copies)
    total, write_list = tables(layout, ext_ref, near_ref, item_ref, keep_ref, last_ref)
    own_ref[0] = total.astype(jnp.float32)

    def moved(index, target):
        return pltpu.make_async_remote_copy(
            src_ref=own_ref,
            dst_ref=all_ref.at[pl.ds(index, 1)],
            send_sem=send_all.at[target],
            recv_sem=recv_all.at[index],
            device_id=peers.numbered(target),
            device_id_type=MESH,
        )

    peers.others(lambda number: moved(peers.me, number).start())
    all_ref[pl.ds(peers.me, 1)] = own_ref[...]
    write_list()
    peers.others(lambda number: moved(number, number).wait_recv())
    peers.others(lambda number: moved(number, number).wait_send())
    most_ref[...] = jnp.max(all_ref[...], axis=0).astype(jnp.int32)


def first_exchange(layout, *operands):
    sides = len(layout.sides)
    lanes = layout.per_block
    blocks = layout.blocks
    total = math.prod(layout.counts)
    height = layout.list_size // lanes
    anywhere = pl.BlockSpec(memory_space=pl.ANY)
    return pl.pallas_call(
        functools.partial(first_kernel, layout),
        out_shape=[
            jax.ShapeDtypeStruct((layout.dead + 1, 3, 4, lanes), jnp.float32),
            jax.ShapeDtypeStruct((4 * blocks, lanes), jnp.int32),
            jax.ShapeDtypeStruct((2, height, lanes), jnp.int32),
            jax.ShapeDtypeStruct((height, lanes), jnp.float32),
            jax.ShapeDtypeStruct((1, lanes), jnp.int32),
            jax.ShapeDtypeStruct((1, lanes), jnp.int32),
        ],
        in_specs=[anywhere] * 5 + [SMEM] * 5,
        out_specs=[VMEM] * 6,
        scratch_shapes=[
            pltpu.VMEM((blocks, 3, 1, lanes), jnp.float32),
            pltpu.VMEM((blocks, 3, 1, lanes), jnp.float32),
            pltpu.VMEM((blocks, lanes), jnp.float32),
            pltpu.VMEM((blocks, lanes), jnp.float32),
            pltpu.VMEM((blocks, lanes), jnp.int32),
            pltpu.VMEM((blocks, 3, 4, lanes), jnp.float32),
            pltpu.VMEM((1, 1, lanes), jnp.float32),
            pltpu.VMEM((total, 1, lanes), jnp.float32),
            pltpu.SemaphoreType.DMA((5,)),
            pltpu.SemaphoreType.DMA((sides,)),
            pltpu.SemaphoreType.DMA((sides,)),
            pltpu.SemaphoreType.DMA((total,)),
            pltpu.SemaphoreType.DMA((total,)),
        ],
        compiler_params=pltpu.CompilerParams(
            collective_id=1, has_side_effects=True, vmem_limit_bytes=VMEM_FIRST
        ),
    )(*operands)


def pair_terms(place, partner, force, adjoint):
    d = [place("position", axis) - partner("position", axis) for axis in range(3)]
    s = d[0] * d[0] + d[1] * d[1] + d[2] * d[2]
    sigma = place("sigma") + partner("sigma")
    square = sigma * sigma
    inverse = 1.0 / (s + square)
    t = square * inverse
    t3 = t * t * t
    soft = s + SOFT
    r = lax.rsqrt(soft)
    b = jnp.exp2(EXPONENT * (soft * r)) * r
    c = jnp.maximum(1.0 - s, 0.0)
    cc = c * c
    p = c * inverse
    y = c * r
    et = place("depth") * partner("depth") * t3
    below = t3 - 1.0
    twice = t3 + below
    half = 1.0 + 0.5 * r
    k1 = 3.0 + y * half
    charge_b = partner("charge") * b
    qb = place("charge") * charge_b
    g1 = cc * (et * (below + p * twice) + qb * k1)
    terms = [g1 * d[axis] for axis in range(3)] if force else []
    if not adjoint:
        return terms, []
    h = p * (p * (7.0 * t3 - 2.0) + 3.0 * twice) + below
    k2 = y * (y * (1.0 + r * (1.5 + 0.75 * r)) + 6.0 * half) + 6.0
    k = -2.0 * c * (2.0 * et * h + qb * k2)
    return terms, [g1, k, cc * k1 * charge_b]


def pulled_terms(place, partner, g1, k, m):
    d = [place("position", axis) - partner("position", axis) for axis in range(3)]
    delta = [place("cotangent", axis) - partner("cotangent", axis) for axis in range(3)]
    along = delta[0] * d[0] + delta[1] * d[1] + delta[2] * d[2]
    ka = k * along
    return [g1 * delta[axis] + ka * d[axis] for axis in range(3)] + [m * along]


ROW_AT = {"charge": 0, "sigma": 1, "depth": 2, "position": 3, "cotangent": 6}
TILE_AT = {"charge": 0, "sigma": 1, "depth": 2, "position": 4, "cotangent": 8}


def main_kernel(
    layout,
    trips,
    near_ref,
    item_ref,
    keep_ref,
    last_ref,
    ext_ref,
    vel_ref,
    mass_ref,
    pos_cot_ref,
    vel_cot_ref,
    pos_out,
    vel_out,
    gpos_out,
    gvel_out,
    charge_out,
    own_ref,
    land_ref,
    work_ref,
    shift_ref,
    place_ref,
    past_ref,
    tile_ref,
    row_ref,
    sum_ref,
    send_sem,
    recv_sem,
):
    blocks, depth, groups, lanes = layout.blocks, layout.depth, layout.groups, layout.per_block
    tiles = blocks * depth
    dead_row = blocks * groups
    peers = Peers(layout)
    lane = lax.broadcasted_iota(jnp.int32, (4, lanes), 1)
    row4 = lax.broadcasted_iota(jnp.int32, (4, lanes), 0)

    for number, d in enumerate(CUBE):
        value = jnp.zeros((4, lanes), jnp.float32)
        for axis in range(3):
            value = jnp.where(row4 == axis, float(d[axis]), value)
        shift_ref[number] = value

    def spread_rows(first, values, scales=(1.0, 1.0, 1.0)):
        for j, value in enumerate(values):
            turned = jnp.concatenate([value, value], axis=0).T
            for part in range(3):
                wide = jnp.broadcast_to(turned[:, part : part + 1], (lanes, lanes))
                if scales[part] != 1.0:
                    wide = wide * scales[part]
                row_ref[j * groups : (j + 1) * groups, first + part] = wide.reshape(
                    groups, GROUP, lanes
                )

    def pack(read, first, shifted):
        carried = [jnp.zeros((4, lanes), jnp.float32)] * blocks
        for k in range(depth):
            for j in range(blocks):
                value = read(near_ref[j, k])
                if shifted:
                    value = value + shift_ref[near_ref[blocks + j, k]]
                offset = near_ref[2 * blocks + j, k]
                turned = pltpu.roll(value, offset, 1)
                current = jnp.where(lane >= offset, turned, carried[j])
                tile_ref[j * depth + k, first : first + 4, :] = current
                carried[j] = jnp.where(lane < near_ref[3 * blocks + j, k], turned, current)

    def access(item):
        group = item_ref[item]
        tile = item_ref[layout.list_size + item]

        def place(name, axis=0):
            return row_ref[group, ROW_AT[name] + axis]

        def partner(name, axis=0):
            at = TILE_AT[name] + axis
            return tile_ref[tile, at : at + 1, :]

        return place, partner

    def run(body, wide):
        def batch(index, total):
            base = index * UNROLL
            found = [body(base + sub) for sub in range(UNROLL)]
            for sub in range(UNROLL):
                item = base + sub
                sums, kept = found[sub]
                for part, value in enumerate(kept):
                    sum_ref[item + 1, 3 + part] = value
                keep = keep_ref[item]
                total = tuple(keep * old + new for old, new in zip(total, sums))
                for part, value in enumerate(total):
                    sum_ref[item + 1, part] = value
            return total

        zero = jnp.zeros((GROUP, lanes), jnp.float32)
        lax.fori_loop(0, trips // UNROLL, batch, (zero,) * wide)

    def reduced(wide):
        which = lax.broadcasted_iota(jnp.int32, (lanes, 8), 1)
        result = []
        for j in range(blocks):
            ends = [last_ref[0, j * groups + group] for group in range(groups)]
            columns = jnp.zeros((lanes, 8), jnp.float32)
            for part in range(wide):
                gathered = jnp.concatenate([sum_ref[end, part] for end in ends], axis=0)
                summed = jnp.sum(gathered, axis=1, keepdims=True)
                columns = jnp.where(which == part, summed, columns)
            result.append(columns.T)
        return result

    def force_item(item):
        return pair_terms(*access(item), True, False)

    def both_item(item):
        return pair_terms(*access(item), True, True)

    def coefficient_item(item):
        return pair_terms(*access(item), False, True)

    def pulled_item(item):
        coefficients = [sum_ref[item + 1, 3 + part] for part in range(3)]
        return pulled_terms(*access(item), *coefficients), []

    def read_work(slot):
        return work_ref[slot]

    def arrived(parity):
        work_ref[0:blocks] = own_ref[parity]
        work_ref[blocks : layout.dead] = land_ref[parity]

    def copies_of(parity):
        return peers.copies(
            own_ref.at[parity],
            land_ref.at[parity],
            blocks,
            send_sem.at[parity],
            recv_sem.at[parity],
        )

    zero_four = jnp.zeros((1, lanes), jnp.float32)
    row_ref[dead_row] = jnp.zeros(row_ref.shape[1:], jnp.float32)
    for part in range(sum_ref.shape[1]):
        sum_ref[0, part] = jnp.zeros((GROUP, lanes), jnp.float32)
    spread_rows(ROW_AT["charge"], [ext_ref[j, 1] for j in range(blocks)], (8.0, 1.0, 24.0))
    pack(lambda slot: ext_ref[slot, 1], TILE_AT["charge"], False)
    work_ref[...] = ext_ref[:, 0]
    inverse = [1.0 / mass_ref[j : j + 1, :] for j in range(blocks)]
    for j in range(blocks):
        vel_out[j] = vector_rows(vel_ref, j)
        pos_out[j] = ext_ref[j, 0, 0:3]
        place_ref[0, j] = ext_ref[j, 0]
        gpos_out[j] = vector_rows(pos_cot_ref, j)
        gvel_out[j] = vector_rows(vel_cot_ref, j)
        charge_out[j] = jnp.zeros((1, lanes), jnp.float32)
    spread_rows(ROW_AT["position"], [work_ref[j] for j in range(blocks)])
    at_position = pl.ds(TILE_AT["position"], 4)
    peers.greet()

    def forward(step, carry):
        pack(read_work, TILE_AT["position"], True)
        for tile in range(tiles):
            past_ref[step, tile] = tile_ref[tile, at_position, :]
        run(force_item, 3)
        force = reduced(3)
        factor = jnp.where(step > 0, TIME_STEP, HALF_STEP)
        parity = lax.rem(step, 2)
        for j in range(blocks):
            velocity = vel_out[j] + factor * inverse[j] * force[j][0:3]
            vel_out[j] = velocity
            position = pos_out[j] + TIME_STEP * velocity
            pos_out[j] = position
            own_ref[parity, j] = jnp.concatenate([position, zero_four], axis=0)
        copies = copies_of(parity)
        start_all(copies)
        for j in range(blocks):
            place_ref[step + 1, j] = own_ref[parity, j]
        spread_rows(ROW_AT["position"], [own_ref[parity, j] for j in range(blocks)])
        wait_all(copies)
        arrived(parity)
        return carry

    lax.fori_loop(0, STEPS, forward, 0)
    pack(read_work, TILE_AT["position"], True)
    run(both_item, 3)
    force = reduced(3)
    for j in range(blocks):
        vel_out[j] = vel_out[j] + HALF_STEP * inverse[j] * force[j][0:3]
    work_ref[...] = ext_ref[:, 2]
    spread_rows(ROW_AT["cotangent"], [work_ref[j] for j in range(blocks)])

    def backward(index, carry):
        step = STEPS - index
        pack(read_work, TILE_AT["cotangent"], False)
        run(pulled_item, 4)
        pulled = reduced(4)
        for j in range(blocks):
            gpos_out[j] = gpos_out[j] + pulled[j][0:3]
            charge_out[j] = charge_out[j] + pulled[j][3:4]

        @pl.when(index < STEPS)
        def _():
            factor = jnp.where(step > 1, TIME_STEP, HALF_STEP)
            parity = lax.rem(index + STEPS, 2)
            for j in range(blocks):
                grad = gvel_out[j] + TIME_STEP * gpos_out[j]
                gvel_out[j] = grad
                own_ref[parity, j] = jnp.concatenate(
                    [factor * inverse[j] * grad, zero_four], axis=0
                )
            copies = copies_of(parity)
            start_all(copies)
            spread_rows(ROW_AT["cotangent"], [own_ref[parity, j] for j in range(blocks)])
            spread_rows(ROW_AT["position"], [place_ref[step - 1, j] for j in range(blocks)])
            for tile in range(tiles):
                tile_ref[tile, at_position, :] = past_ref[step - 1, tile]
            run(coefficient_item, 0)
            wait_all(copies)
            arrived(parity)

        return carry

    lax.fori_loop(0, STEPS + 1, backward, 0)
    for j in range(blocks):
        alive = lane[0:1] < ext_ref[j, 0, 3:4].astype(jnp.int32)
        charge_out[j] = jnp.where(alive, 8.0 * charge_out[j], 0.0)


def integrate(layout, trips, identity, operands):
    blocks, depth, groups, lanes = layout.blocks, layout.depth, layout.groups, layout.per_block
    sides = len(layout.sides)
    rows = blocks * groups + 1
    vector = jax.ShapeDtypeStruct((blocks, 3, lanes), jnp.float32)
    return pl.pallas_call(
        functools.partial(main_kernel, layout, trips),
        out_shape=[vector] * 4 + [jax.ShapeDtypeStruct((blocks, 1, lanes), jnp.float32)],
        in_specs=[SMEM] * 4 + [VMEM] * 5,
        out_specs=[VMEM] * 5,
        scratch_shapes=[
            pltpu.VMEM((2, blocks, 4, lanes), jnp.float32),
            pltpu.VMEM((2, layout.dead - blocks, 4, lanes), jnp.float32),
            pltpu.VMEM((layout.dead + 1, 4, lanes), jnp.float32),
            pltpu.VMEM((len(CUBE), 4, lanes), jnp.float32),
            pltpu.VMEM((STEPS + 1, blocks, 4, lanes), jnp.float32),
            pltpu.VMEM((STEPS, blocks * depth, 4, lanes), jnp.float32),
            pltpu.VMEM((blocks * depth, 16, lanes), jnp.float32),
            pltpu.VMEM((rows, 9, GROUP, lanes), jnp.float32),
            pltpu.VMEM((trips + 1, 6, GROUP, lanes), jnp.float32),
            pltpu.SemaphoreType.DMA((2, sides)),
            pltpu.SemaphoreType.DMA((2, sides)),
        ],
        compiler_params=pltpu.CompilerParams(
            collective_id=identity, has_side_effects=True, vmem_limit_bytes=52 * 1024 * 1024
        ),
    )(*operands)


def store_kernel(*refs):
    for source, target in zip(refs[: len(refs) // 2], refs[len(refs) // 2 :]):
        for j in range(source.shape[0]):
            for axis in range(source.shape[1]):
                target[j, axis] = source[j, axis : axis + 1, :]


def stored(values):
    return pl.pallas_call(
        store_kernel,
        out_shape=[
            jax.ShapeDtypeStruct(value.shape[:2] + (1, value.shape[2]), value.dtype)
            for value in values
        ],
        in_specs=[VMEM] * len(values),
        out_specs=[VMEM] * len(values),
        compiler_params=pltpu.CompilerParams(vmem_limit_bytes=60 * 1024 * 1024),
    )(*values)


def classes(most):
    return [-(-most * part // 32 // UNROLL) * UNROLL for part in (10, 12, 13, 14, 16, 32)]


def on_device(
    positions,
    velocities,
    charges,
    atom_types,
    atom_count,
    sigma_type,
    epsilon_type,
    masses,
    pair_list,
    pair_count,
    pos_cotangent,
    vel_cotangent,
):
    own = positions.shape[:3]
    lanes = positions.shape[-1]
    layout = Layout(tuple(lax.axis_size(axis) for axis in AXES), own, lanes)
    blocks = layout.blocks

    def flat(array):
        return array.reshape((blocks,) + array.shape[3:])

    def upright(array):
        return array.reshape(blocks, 3, 1, lanes)

    mass, cotangent = flat(masses), upright(vel_cotangent)
    extended, near, items, keep, last, most = first_exchange(
        layout,
        upright(positions),
        cotangent,
        mass,
        flat(charges),
        flat(atom_types),
        flat(atom_count),
        sigma_type,
        epsilon_type,
        pair_list[0, 0, 0],
        pair_count.reshape(1),
    )
    items, keep, most = items.reshape(-1), keep.reshape(-1), most[0, 0]
    sizes = classes(layout.most_items)
    which = sum((most > size).astype(jnp.int32) for size in sizes[:-1])
    operands = (near, items, keep, last, extended, upright(velocities), mass, upright(pos_cotangent), cotangent)
    branches = [
        functools.partial(integrate, layout, size, 2 + index) for index, size in enumerate(sizes)
    ]
    out = stored(lax.switch(which, branches, operands))
    shapes = [positions.shape] * 4 + [charges.shape]
    return tuple(value.reshape(shape) for value, shape in zip(out, shapes))


def solution(mesh):
    block = P("gx", "gy", "gz")
    in_specs = (block,) * 5 + (P(), P()) + (block,) * 5
    return jax.shard_map(
        on_device, mesh=mesh, in_specs=in_specs, out_specs=(block,) * 5, check_vma=False
    )
```
